32 devices in a mesh: groups: 2 (over y), slab: 4 (over z), batch: 2 (over x), chan: 2 (over core).
Axes of the slice: x: 2, y: 2, z: 4, core: 2. Of those that a mesh axis runs over, the one named last changes fastest.
Arguments:
- volume: bfloat16 [16, 8, 4, 8, 128], P(('groups', 'batch'), 'slab'), parts along dimension 0, may hold values from -6 to 6
- targets: float32 [16, 4], P(('groups', 'batch')), parts along dimension 0, may hold values from -1 to 1
- front_weight: bfloat16 [3, 3, 3, 128, 128], P(None, None, None, None, 'chan'), may hold values from -0.109375 to 0.109375
- stride_weight: bfloat16 [3, 3, 3, 128, 256], P(None, None, None, 'chan'), may hold values from -0.109375 to 0.109375
- hidden_weight: float32 [256, 128], P('chan'), may hold values from -0.375 to 0.375
- output_weight: float32 [128, 4], replicated, may hold values from -0.5 to 0.5
Outputs:
- grad_front: float32 [6, 3, 3, 128, 128], P('groups', None, None, None, 'chan'), parts along dimension 0
- grad_stride: float32 [6, 3, 3, 128, 256], P('groups', None, None, 'chan'), parts along dimension 0
- grad_hidden: float32 [512, 128], P(('groups', 'chan')), parts along dimension 0
- grad_output: float32 [256, 4], P('groups'), parts along dimension 0
- loss: float32 [2], P('groups'), parts along dimension 0
The draws below stay inside these ranges and needn't reach their ends.
There are 2 independent parts, one for each index of `groups`. The reference program is written for one: setup_inputs(seed, part) draws one part's arguments, and reference() takes and returns one part's arrays. A program takes and returns all parts, laid end to end along the dimension named above; an argument that names none is the same for every part. Nothing has to cross between parts.
All inputs are finite; a program needn't handle non-finite values.
Results may differ from the reference program's by a relative error of at most 0.0052.
Values may be sent and summed in bfloat16 or wider, within the bound.
A program may use at most 64 MiB of HBM per device.

```python
import jax
import jax.numpy as jnp
from jax import lax

C1 = 128
C2 = 256
HID = 128
OUTS = 4
XW = 4
YW = 8
ZD = 8
SAMPLES = 8
Z2 = 4
X2 = 2
Y2 = 4
CELLS2 = 32


def level_of(rng, extent, pieces, smallest, top_value):
    loudness = 1.0
    for position, blocks in pieces:
        draws = jax.random.uniform(jax.random.fold_in(jax.random.fold_in(rng, 6), position), (blocks,), jnp.float32, smallest / len(pieces), top_value / len(pieces))
        loudness = loudness * jnp.repeat(jnp.exp(draws), extent[position] // blocks).reshape((-1,) + (1,) * (len(extent) - 1 - position))
    return loudness


def scatter_about(rng, dims, deviation, reach, cuts=(), kind=jnp.bfloat16):
    array = jax.random.normal(rng, dims, jnp.float32) * deviation
    if len(cuts) > 0:
        array = level_of(rng, dims, cuts, -0.22, 0.18) * array
    return jnp.clip(array, min=-reach, max=reach).astype(kind)


def setup_inputs(seed: int = 0, part: int = 0) -> dict:
    key_of = jax.random.split(jax.random.key(seed), 7)
    part_keys = jax.random.split(jax.random.fold_in(key_of[6], part), 7)
    volume = scatter_about(part_keys[0], (SAMPLES, ZD, XW, YW, C1), 1.0, 6.0, ((0, 2), (1, 4)))
    targets = jnp.clip(jax.random.uniform(part_keys[1], (SAMPLES, OUTS), jnp.float32, -1.0, 1.0) * level_of(part_keys[1], (SAMPLES, OUTS), ((0, 2),), -0.4, 0.0), -1.0, 1.0)
    front_weight = scatter_about(key_of[2], (3, 3, 3, C1, C1), (27 * C1) ** -0.5, 0.109375, ((4, 2),))
    stride_weight = scatter_about(key_of[3], (3, 3, 3, C1, C2), (27 * C1) ** -0.5, 0.109375, ((3, 2),))
    hidden_weight = scatter_about(key_of[4], (C2, HID), C2 ** -0.5, 0.375, ((0, 2),), jnp.float32)
    output_weight = scatter_about(key_of[5], (HID, OUTS), HID ** -0.5, 0.5, (), jnp.float32)
    return {"volume": volume, "targets": targets, "front_weight": front_weight, "stride_weight": stride_weight, "hidden_weight": hidden_weight, "output_weight": output_weight}


def swish_slope(preact):
    logistic = jax.nn.sigmoid(preact)
    return logistic * (1.0 + preact * (1.0 - logistic))

def tap_window(padded, tap_z, tap_x, tap_y, extent_z, extent_x, extent_y, stride):
    if stride == 1:
        return padded[:, tap_z:tap_z + extent_z, tap_x:tap_x + extent_x, tap_y:tap_y + extent_y, :]
    leading = padded.shape[0]
    channels = padded.shape[-1]
    folded = padded.reshape(leading, extent_z + 1, 2, extent_x + 1, 2, extent_y + 1, 2, channels)
    return folded[:, tap_z // 2:tap_z // 2 + extent_z, tap_z % 2, tap_x // 2:tap_x // 2 + extent_x, tap_x % 2, tap_y // 2:tap_y // 2 + extent_y, tap_y % 2, :]

def conv_apply(padded, weight, extent_z, extent_x, extent_y, stride):
    summed = None
    for tap_z in range(3):
        for tap_x in range(3):
            for tap_y in range(3):
                window = tap_window(padded, tap_z, tap_x, tap_y, extent_z, extent_x, extent_y, stride)
                flat_tap = window.reshape(-1, window.shape[-1])
                contrib = jnp.dot(flat_tap, weight[tap_z, tap_x, tap_y], preferred_element_type=jnp.float32)
                summed = contrib if summed is None else summed + contrib
    return summed.reshape(padded.shape[0], extent_z, extent_x, extent_y, weight.shape[-1])

def kernel_grad(padded, grad_out, extent_z, extent_x, extent_y, stride):
    flat_grad = grad_out.reshape(-1, grad_out.shape[-1])
    results = []
    for tap_z in range(3):
        for tap_x in range(3):
            for tap_y in range(3):
                window = tap_window(padded, tap_z, tap_x, tap_y, extent_z, extent_x, extent_y, stride)
                flat_tap = window.reshape(-1, window.shape[-1])
                results.append(lax.dot_general(flat_tap, flat_grad, (((0,), (0,)), ((), ())), preferred_element_type=jnp.float32))
    return jnp.stack(results).reshape(3, 3, 3, padded.shape[-1], grad_out.shape[-1])

def input_grad(grad_out, weight, extent_z, extent_x, extent_y):
    leading = grad_out.shape[0]
    channels = weight.shape[3]
    flat_grad = grad_out.reshape(-1, grad_out.shape[-1])
    buckets = {}
    for tap_z in range(3):
        for tap_x in range(3):
            for tap_y in range(3):
                contrib = lax.dot_general(flat_grad, weight[tap_z, tap_x, tap_y], (((1,), (1,)), ((), ())), preferred_element_type=jnp.float32)
                contrib = contrib.reshape(leading, extent_z, extent_x, extent_y, channels)
                placed = jnp.pad(contrib, ((0, 0), (tap_z // 2, 1 - tap_z // 2), (tap_x // 2, 1 - tap_x // 2), (tap_y // 2, 1 - tap_y // 2), (0, 0)))
                parity = (tap_z % 2, tap_x % 2, tap_y % 2)
                buckets[parity] = placed if parity not in buckets else buckets[parity] + placed
    planes_z = []
    for par_z in range(2):
        planes_x = []
        for par_x in range(2):
            planes_x.append(jnp.stack([buckets[par_z, par_x, par_y] for par_y in range(2)], axis=4))
        planes_z.append(jnp.stack(planes_x, axis=3))
    assembled = jnp.stack(planes_z, axis=2)
    assembled = assembled.reshape(leading, 2 * extent_z + 2, 2 * extent_x + 2, 2 * extent_y + 2, channels)
    return assembled[:, 1:-1, 1:-1, 1:-1, :]

def reference(volume, targets, front_weight, stride_weight, hidden_weight, output_weight):
    highest = lax.Precision.HIGHEST
    padded = jnp.pad(volume, ((0, 0), (1, 1), (1, 1), (1, 1), (0, 0)))
    front_pre = conv_apply(padded, front_weight, ZD, XW, YW, 1)
    front_act = jax.nn.silu(front_pre).astype(jnp.bfloat16)
    stride_pad = jnp.pad(front_act, ((0, 0), (1, 1), (1, 1), (1, 1), (0, 0)))
    stride_pre = conv_apply(stride_pad, stride_weight, Z2, X2, Y2, 2)
    pooled = lax.optimization_barrier(jnp.sum(jax.nn.silu(stride_pre), axis=(1, 2, 3))) / CELLS2
    hidden_pre = jnp.dot(pooled, hidden_weight, precision=highest)
    hidden_act = jax.nn.silu(hidden_pre)
    predicted = jnp.dot(hidden_act, output_weight, precision=highest)
    residual = predicted - targets
    grad_output = jnp.dot(hidden_act.T, residual, precision=highest)
    grad_hidden_pre = jnp.dot(residual, output_weight.T, precision=highest) * swish_slope(hidden_pre)
    grad_hidden = jnp.dot(pooled.T, grad_hidden_pre, precision=highest)
    grad_pooled = jnp.dot(grad_hidden_pre, hidden_weight.T, precision=highest)
    grad_stride_pre = (grad_pooled[:, None, None, None, :] / CELLS2 * swish_slope(stride_pre)).astype(jnp.bfloat16)
    grad_stride = kernel_grad(stride_pad, grad_stride_pre, Z2, X2, Y2, 2)
    grad_act = input_grad(grad_stride_pre, stride_weight, Z2, X2, Y2).astype(jnp.bfloat16)
    grad_front_pre = (grad_act * swish_slope(front_pre)).astype(jnp.bfloat16)
    grad_front = kernel_grad(padded, grad_front_pre, ZD, XW, YW, 1)
    loss = (jnp.sum(residual * residual) / (SAMPLES * OUTS)).reshape(1)
    return (grad_front, grad_stride, grad_hidden, grad_output, loss)
```

```python
import functools

import jax
import jax.numpy as jnp
from jax import lax
from jax.experimental import pallas as pl
from jax.experimental.pallas import tpu as pltpu
from jax.sharding import PartitionSpec as P


def with_halo(cells, sides, width):
    for axis, dim in sides:
        count = lax.axis_size(axis)
        ends = count - 1
        head = lax.slice_in_dim(cells, 0, width, axis=dim)
        tail = lax.slice_in_dim(cells, cells.shape[dim] - width, cells.shape[dim], axis=dim)
        cells = jnp.concatenate(
            [
                lax.ppermute(tail, axis, [(i, (i + 1) % count) for i in range(ends)]),
                cells,
                lax.ppermute(head, axis, [((i + 1) % count, i) for i in range(ends)]),
            ],
            axis=dim,
        )
    return cells


def swish_slope(preact):
    logistic = jax.nn.sigmoid(preact)
    return logistic * (1.0 + preact * (1.0 - logistic))


def tap_window(padded, tap_z, tap_x, tap_y, extent_z, extent_x, extent_y, stride):
    if stride == 1:
        return padded[
            :, tap_z : tap_z + extent_z, tap_x : tap_x + extent_x, tap_y : tap_y + extent_y, :
        ]
    leading = padded.shape[0]
    channels = padded.shape[-1]
    folded = padded.reshape(leading, extent_z + 1, 2, extent_x + 1, 2, extent_y + 1, 2, channels)
    return folded[
        :,
        tap_z // 2 : tap_z // 2 + extent_z,
        tap_z % 2,
        tap_x // 2 : tap_x // 2 + extent_x,
        tap_x % 2,
        tap_y // 2 : tap_y // 2 + extent_y,
        tap_y % 2,
        :,
    ]


def conv_apply(padded, weight, extent_z, extent_x, extent_y, stride):
    summed = None
    for tap_z in range(3):
        for tap_x in range(3):
            for tap_y in range(3):
                window = tap_window(
                    padded, tap_z, tap_x, tap_y, extent_z, extent_x, extent_y, stride
                )
                flat_tap = window.reshape(-1, window.shape[-1])
                contrib = jnp.dot(
                    flat_tap, weight[tap_z, tap_x, tap_y], preferred_element_type=jnp.float32
                )
                summed = contrib if summed is None else summed + contrib
    return summed.reshape(padded.shape[0], extent_z, extent_x, extent_y, weight.shape[-1])


def kernel_grad(padded, grad_out, extent_z, extent_x, extent_y, stride):
    flat_grad = grad_out.reshape(-1, grad_out.shape[-1])
    results = []
    for tap_z in range(3):
        for tap_x in range(3):
            for tap_y in range(3):
                window = tap_window(
                    padded, tap_z, tap_x, tap_y, extent_z, extent_x, extent_y, stride
                )
                flat_tap = window.reshape(-1, window.shape[-1])
                results.append(
                    lax.dot_general(
                        flat_tap,
                        flat_grad,
                        (((0,), (0,)), ((), ())),
                        preferred_element_type=jnp.float32,
                    )
                )
    return jnp.stack(results).reshape(3, 3, 3, padded.shape[-1], grad_out.shape[-1])


def input_grad(grad_out, weight, extent_z, extent_x, extent_y):
    leading = grad_out.shape[0]
    channels = weight.shape[3]
    flat_grad = grad_out.reshape(-1, grad_out.shape[-1])
    buckets = {}
    for tap_z in range(3):
        for tap_x in range(3):
            for tap_y in range(3):
                contrib = lax.dot_general(
                    flat_grad,
                    weight[tap_z, tap_x, tap_y],
                    (((1,), (1,)), ((), ())),
                    preferred_element_type=jnp.float32,
                )
                contrib = contrib.reshape(leading, extent_z, extent_x, extent_y, channels)
                placed = jnp.pad(
                    contrib,
                    (
                        (0, 0),
                        (tap_z // 2, 1 - tap_z // 2),
                        (tap_x // 2, 1 - tap_x // 2),
                        (tap_y // 2, 1 - tap_y // 2),
                        (0, 0),
                    ),
                )
                parity = (tap_z % 2, tap_x % 2, tap_y % 2)
                buckets[parity] = placed if parity not in buckets else buckets[parity] + placed
    planes_z = []
    for par_z in range(2):
        planes_x = []
        for par_x in range(2):
            planes_x.append(jnp.stack([buckets[par_z, par_x, par_y] for par_y in range(2)], axis=4))
        planes_z.append(jnp.stack(planes_x, axis=3))
    assembled = jnp.stack(planes_z, axis=2)
    assembled = assembled.reshape(
        leading, 2 * extent_z + 2, 2 * extent_x + 2, 2 * extent_y + 2, channels
    )
    return assembled[:, 1:-1, 1:-1, 1:-1, :]


def split_body(volume, targets, front_weight, stride_weight, hidden_weight, output_weight):
    highest = lax.Precision.HIGHEST
    slabs = lax.axis_size("slab")
    batches = lax.axis_size("batch")
    inner = front_weight.shape[-1]
    leading, thick, extent_x, extent_y, channels = volume.shape
    depth = thick * slabs
    outputs = output_weight.shape[-1]
    haloed = with_halo(volume, (("slab", 1),), 1)
    padded = jnp.pad(haloed, ((0, 0), (0, 0), (1, 1), (1, 1), (0, 0)))
    front_pre = conv_apply(padded, front_weight, thick, extent_x, extent_y, 1)
    front_act = jax.nn.silu(front_pre).astype(jnp.bfloat16)
    merged = front_act.reshape(leading, thick, extent_x, extent_y * inner)
    sample_act = lax.all_to_all(merged, "slab", split_axis=0, concat_axis=1, tiled=True)
    sample_act = sample_act.reshape(1, depth, extent_x, extent_y, inner)
    half_z = depth // 2
    half_x = extent_x // 2
    half_y = extent_y // 2
    cells = half_z * half_x * half_y
    stride_pad = jnp.pad(sample_act, ((0, 0), (1, 1), (1, 1), (1, 1), (0, 0)))
    partial_pre = conv_apply(stride_pad, stride_weight, half_z, half_x, half_y, 2)
    stride_pre = lax.psum_scatter(partial_pre, "chan", scatter_dimension=4, tiled=True)
    pooled = jnp.sum(jax.nn.silu(stride_pre), axis=(0, 1, 2, 3)) / cells
    hidden_pre = lax.psum(jnp.dot(pooled, hidden_weight, precision=highest), "chan")
    hidden_act = jax.nn.silu(hidden_pre)
    predicted = jnp.dot(hidden_act, output_weight, precision=highest)
    target_row = lax.dynamic_index_in_dim(targets, lax.axis_index("slab"), 0, keepdims=False)
    residual = predicted - target_row
    squared = jnp.sum(residual * residual)
    grad_output = jnp.outer(hidden_act, residual)
    grad_hidden_pre = jnp.dot(output_weight, residual, precision=highest) * swish_slope(hidden_pre)
    grad_hidden = jnp.outer(pooled, grad_hidden_pre)
    grad_pooled = jnp.dot(hidden_weight, grad_hidden_pre, precision=highest)
    grad_stride_pre = (grad_pooled / cells * swish_slope(stride_pre)).astype(jnp.bfloat16)
    full_grad = lax.all_gather(grad_stride_pre, "chan", axis=4, tiled=True)
    grad_stride = kernel_grad(stride_pad, full_grad, half_z, half_x, half_y, 2)
    grad_act = input_grad(full_grad, stride_weight, half_z, half_x, half_y).astype(jnp.bfloat16)
    returned = lax.all_to_all(
        grad_act.reshape(1, depth, extent_x, extent_y * inner),
        "slab",
        split_axis=1,
        concat_axis=0,
        tiled=True,
    )
    returned = returned.reshape(leading, thick, extent_x, extent_y, inner)
    grad_front_pre = (returned * swish_slope(front_pre)).astype(jnp.bfloat16)
    grad_front = kernel_grad(padded, grad_front_pre, thick, extent_x, extent_y, 1)
    grad_front, grad_stride, grad_hidden, grad_output, squared = lax.psum(
        (grad_front, grad_stride, grad_hidden, grad_output, squared), ("slab", "batch")
    )
    loss = (squared / (slabs * batches * outputs)).reshape(1)
    return (grad_front, grad_stride, grad_hidden, grad_output, loss)


GATHER_LIMIT = 1 << 20


def whole_kernel(
    shape,
    volume_ref, targets_ref, front_own_ref, front_other_ref, stride_ref, hidden_ref, output_ref,
    grad_front_ref, grad_stride_ref, grad_hidden_ref, grad_output_ref, loss_ref,
    taps_ref, front_ref, act_ref, slope_ref, strided_ref, spread_ref, grad_pre_ref,
):
    slabs, batches, leading, thick, extent_x, extent_y, channels, inner = shape
    f32, bf16 = jnp.float32, jnp.bfloat16
    highest = lax.Precision.HIGHEST
    samples = batches * leading
    depth = slabs * thick
    rows = samples * extent_y
    half_z, half_x, half_y = depth // 2, extent_x // 2, extent_y // 2
    half_rows = samples * half_y
    cells = half_z * half_x * half_y
    wide = 3 * channels
    local_rows = leading * extent_y

    front_ref[:, :, :inner] = front_own_ref[...]
    front_ref[:, :, inner:] = front_other_ref[...]

    zeros = jnp.zeros((rows, wide), bf16)
    for x in range(extent_x + 2):
        taps_ref[0, x] = zeros
        taps_ref[depth + 1, x] = zeros

    row = lax.broadcasted_iota(jnp.int32, (rows, channels), 0)
    first = (row & (extent_y - 1)) == 0
    last = (row & (extent_y - 1)) == extent_y - 1
    half_row = lax.broadcasted_iota(jnp.int32, (half_rows, channels), 0)
    half_first = (half_row & (half_y - 1)) == 0
    half_last = (half_row & (half_y - 1)) == half_y - 1

    def fill(slab, carry):
        for plane in range(thick):
            z = slab * thick + plane
            taps_ref[z + 1, 0] = zeros
            taps_ref[z + 1, extent_x + 1] = zeros
            for x in range(extent_x):
                mid = jnp.concatenate(
                    [
                        volume_ref[b * slabs + slab, :, plane, x].astype(f32).reshape(local_rows, channels)
                        for b in range(batches)
                    ],
                    axis=0,
                )
                low = jnp.where(first, 0.0, pltpu.roll(mid, 1, 0))
                high = jnp.where(last, 0.0, pltpu.roll(mid, rows - 1, 0))
                taps_ref[z + 1, x + 1, :, :channels] = low.astype(bf16)
                taps_ref[z + 1, x + 1, :, channels : 2 * channels] = mid.astype(bf16)
                taps_ref[z + 1, x + 1, :, 2 * channels :] = high.astype(bf16)
        return carry

    lax.fori_loop(0, slabs, fill, 0)

    half_zeros = jnp.zeros((half_rows, wide), bf16)
    for x in range(extent_x + 1):
        strided_ref[0, x] = half_zeros

    def front(z, carry):
        total = jnp.zeros((extent_x * rows, channels), f32)
        for kz in range(3):
            for kx in range(3):
                window = taps_ref[z + kz, kx : kx + extent_x].reshape(extent_x * rows, wide)
                kernel = front_ref[3 * (3 * kz + kx) : 3 * (3 * kz + kx) + 3].reshape(wide, channels)
                total += jnp.dot(window, kernel, preferred_element_type=f32)
        logistic = 1.0 / (1.0 + jnp.exp(-total))
        act = (total * logistic).astype(bf16).astype(f32)
        slope = logistic * (1.0 + total * (1.0 - logistic))
        act_ref[z] = act.reshape(extent_x, rows, channels)
        slope_ref[z] = slope.reshape(extent_x, rows, channels)
        strided_ref[z + 1, 0] = half_zeros
        for x in range(extent_x):
            even = act_ref[z, x, pl.ds(0, half_rows, stride=2), :]
            odd = act_ref[z, x, pl.ds(1, half_rows, stride=2), :]
            low = jnp.where(half_first, 0.0, pltpu.roll(odd, 1, 0))
            strided_ref[z + 1, x + 1, :, :channels] = low.astype(bf16)
            strided_ref[z + 1, x + 1, :, channels : 2 * channels] = even.astype(bf16)
            strided_ref[z + 1, x + 1, :, 2 * channels :] = odd.astype(bf16)
        return carry

    lax.fori_loop(0, depth, front, 0)

    def strided_window(kz, kx):
        return jnp.concatenate(
            [strided_ref[kz + 2 * z, kx + 2 * x] for z in range(half_z) for x in range(half_x)], axis=0
        )

    def stride_kernel(kz, kx):
        start = 3 * (3 * kz + kx)
        return stride_ref[start : start + 3].reshape(wide, stride_ref.shape[-1])

    pre = None
    for kz in range(3):
        for kx in range(3):
            term = jnp.dot(strided_window(kz, kx), stride_kernel(kz, kx), preferred_element_type=f32)
            pre = term if pre is None else pre + term
    logistic = 1.0 / (1.0 + jnp.exp(-pre))
    planes = half_z * half_x
    features = pre.shape[-1]
    summed = jnp.sum((pre * logistic).reshape(planes, half_rows, features), axis=0)
    owner = lax.broadcasted_iota(jnp.int32, (samples, half_rows), 1)
    sample = lax.broadcasted_iota(jnp.int32, (samples, half_rows), 0)
    member = ((owner >= sample * half_y) & (owner < (sample + 1) * half_y)).astype(f32)
    pooled = jnp.dot(member, summed, precision=highest, preferred_element_type=f32) / cells
    hidden = hidden_ref[...]
    output = output_ref[...]

    def contract(left, right, dims):
        return lax.dot_general(left, right, (dims, ((), ())), precision=highest, preferred_element_type=f32)

    hidden_pre = contract(pooled, hidden, ((1,), (0,)))
    hidden_logistic = 1.0 / (1.0 + jnp.exp(-hidden_pre))
    hidden_act = hidden_pre * hidden_logistic
    residual = contract(hidden_act, output, ((1,), (0,))) - targets_ref[...]
    loss_ref[...] = jnp.sum(residual * residual, keepdims=True) / (samples * output.shape[-1])
    grad_output_ref[...] = contract(hidden_act, residual, ((0,), (0,)))
    hidden_slope = hidden_logistic * (1.0 + hidden_pre * (1.0 - hidden_logistic))
    grad_hidden_pre = contract(residual, output, ((1,), (1,))) * hidden_slope
    share = features // 2
    pooled_own = jnp.where(lax.axis_index("chan") == 0, pooled[:, :share], pooled[:, share:])
    grad_hidden_ref[...] = contract(pooled_own, grad_hidden_pre, ((0,), (0,)))
    grad_pooled = contract(grad_hidden_pre, hidden, ((1,), (1,)))
    grad_rows = contract(member, grad_pooled, ((0,), (0,))) / cells
    slope = logistic * (1.0 + pre * (1.0 - logistic))
    grad_pre = (slope.reshape(planes, half_rows, features) * grad_rows[None]).astype(bf16)
    grad_pre = grad_pre.reshape(planes * half_rows, features)

    for kz in range(3):
        for kx in range(3):
            start = 3 * (3 * kz + kx)
            spread = lax.dot_general(
                grad_pre, stride_kernel(kz, kx), (((1,), (1,)), ((), ())), preferred_element_type=f32
            )
            spread_ref[3 * kz + kx] = spread.reshape(planes, half_rows, wide)
            kernel = lax.dot_general(
                strided_window(kz, kx), grad_pre, (((0,), (0,)), ((), ())), preferred_element_type=f32
            )
            for ky in range(3):
                grad_stride_ref[start + ky] = kernel[ky * channels : ky * channels + inner]

    def sources(cell, half):
        if cell % 2 == 0:
            return [(1, cell // 2)]
        found = [(2, cell // 2)]
        if cell // 2 + 1 < half:
            found.append((0, cell // 2 + 1))
        return found

    for z in range(depth):
        for x in range(extent_x):
            total = None
            for kz, from_z in sources(z, half_z):
                for kx, from_x in sources(x, half_x):
                    block = spread_ref[3 * kz + kx, from_z * half_x + from_x]
                    total = block if total is None else total + block
            even = total[:, channels : 2 * channels]
            up = jnp.where(half_last, 0.0, pltpu.roll(total[:, :channels], half_rows - 1, 0))
            odd = total[:, 2 * channels :] + up
            for start, grad in ((0, even), (1, odd)):
                grad = grad.astype(bf16).astype(f32)
                place = pl.ds(start, half_rows, stride=2)
                grad_pre_ref[z, x, place, :] = grad * slope_ref[z, x, place, :]

    grads = grad_pre_ref[...].reshape(depth * extent_x * rows, channels).astype(bf16)
    grads = jnp.transpose(grads)[:inner]
    for kz in range(3):
        for kx in range(3):
            window = taps_ref[kz : kz + depth, kx : kx + extent_x]
            window = window.reshape(depth * extent_x * rows, wide)
            turned = jnp.dot(grads, window, preferred_element_type=f32)
            for ky in range(3):
                grad_front_ref[3 * (3 * kz + kx) + ky] = jnp.transpose(
                    turned[:, ky * channels : (ky + 1) * channels]
                )


def whole_batch(shape, features, gathered, targets, front_own, front_other, stride_all, hidden_all, output_weight):
    slabs, batches, leading, thick, extent_x, extent_y, channels, inner = shape
    samples, depth = batches * leading, slabs * thick
    rows = samples * extent_y
    half_rows = rows // 2
    planes = depth * extent_x // 4
    f32, bf16 = jnp.float32, jnp.bfloat16
    outputs = output_weight.shape[-1]
    hid = hidden_all.shape[-1]
    vmem = pl.BlockSpec(memory_space=pltpu.VMEM)
    return pl.pallas_call(
        functools.partial(whole_kernel, shape),
        out_shape=(
            jax.ShapeDtypeStruct((27, channels, inner), f32),
            jax.ShapeDtypeStruct((27, inner, features), f32),
            jax.ShapeDtypeStruct((features // 2, hid), f32),
            jax.ShapeDtypeStruct((hid, outputs), f32),
            jax.ShapeDtypeStruct((1, 1), f32),
        ),
        in_specs=[vmem] * 7,
        out_specs=[vmem] * 5,
        scratch_shapes=[
            pltpu.VMEM((depth + 2, extent_x + 2, rows, 3 * channels), bf16),
            pltpu.VMEM((27, channels, channels), bf16),
            pltpu.VMEM((depth, extent_x, rows, channels), f32),
            pltpu.VMEM((depth, extent_x, rows, channels), f32),
            pltpu.VMEM((depth + 1, extent_x + 1, half_rows, 3 * channels), bf16),
            pltpu.VMEM((9, planes, half_rows, 3 * channels), f32),
            pltpu.VMEM((depth, extent_x, rows, channels), f32),
        ],
        compiler_params=pltpu.CompilerParams(vmem_limit_bytes=48 << 20),
    )(gathered, targets, front_own, front_other, stride_all, hidden_all, output_weight)


def gather_inputs(volume, targets, front_weight, stride_weight, hidden_weight):
    inner = front_weight.shape[-1]
    channels = volume.shape[-1]
    swap = [(0, 1), (1, 0)]
    gathered = lax.all_gather(volume, ("batch", "slab"))
    targets = lax.all_gather(targets, "batch", tiled=True)
    front_own = front_weight.reshape(27, channels, inner)
    stride_own = stride_weight.reshape(27, inner, -1)
    front_other = lax.ppermute(front_own, "chan", swap)
    stride_other = lax.ppermute(stride_own, "chan", swap)
    stride_all = jnp.concatenate([stride_own, stride_other], axis=1)
    hidden_all = lax.all_gather(hidden_weight, "chan", tiled=True)
    return gathered, targets, front_own, front_other, stride_all, hidden_all


def body(volume, targets, front_weight, stride_weight, hidden_weight, output_weight):
    slabs = lax.axis_size("slab")
    batches = lax.axis_size("batch")
    if volume.size * 2 * slabs * batches > GATHER_LIMIT:
        return split_body(volume, targets, front_weight, stride_weight, hidden_weight, output_weight)
    inner = front_weight.shape[-1]
    channels = volume.shape[-1]
    features = stride_weight.shape[-1]
    shape = (slabs, batches) + volume.shape + (inner,)
    gathered = gather_inputs(volume, targets, front_weight, stride_weight, hidden_weight)
    grad_front, grad_stride, grad_hidden, grad_output, loss = whole_batch(
        shape, features, *gathered, output_weight
    )
    return (
        grad_front.reshape(3, 3, 3, channels, inner),
        grad_stride.reshape(3, 3, 3, inner, features),
        grad_hidden,
        grad_output,
        loss.reshape(1),
    )


def solution(mesh):
    in_specs = (
        P(("groups", "batch"), "slab", None, None, None),
        P(("groups", "batch"), None),
        P(None, None, None, None, "chan"),
        P(None, None, None, "chan", None),
        P("chan", None),
        P(),
    )
    out_specs = (
        P("groups", None, None, None, "chan"),
        P("groups", None, None, "chan", None),
        P(("groups", "chan"), None),
        P("groups", None),
        P("groups"),
    )
    return jax.shard_map(body, mesh=mesh, in_specs=in_specs, out_specs=out_specs, check_vma=False)
```

```python
import functools

import jax
import jax.numpy as jnp
from jax import lax
from jax.experimental import pallas as pl
from jax.experimental.pallas import tpu as pltpu
from jax.sharding import PartitionSpec as P


def with_halo(cells, sides, width):
    for axis, dim in sides:
        count = lax.axis_size(axis)
        ends = count - 1
        head = lax.slice_in_dim(cells, 0, width, axis=dim)
        tail = lax.slice_in_dim(cells, cells.shape[dim] - width, cells.shape[dim], axis=dim)
        cells = jnp.concatenate(
            [
                lax.ppermute(tail, axis, [(i, (i + 1) % count) for i in range(ends)]),
                cells,
                lax.ppermute(head, axis, [((i + 1) % count, i) for i in range(ends)]),
            ],
            axis=dim,
        )
    return cells


def swish_slope(preact):
    logistic = jax.nn.sigmoid(preact)
    return logistic * (1.0 + preact * (1.0 - logistic))


def tap_window(padded, tap_z, tap_x, tap_y, extent_z, extent_x, extent_y, stride):
    if stride == 1:
        return padded[
            :, tap_z : tap_z + extent_z, tap_x : tap_x + extent_x, tap_y : tap_y + extent_y, :
        ]
    leading = padded.shape[0]
    channels = padded.shape[-1]
    folded = padded.reshape(leading, extent_z + 1, 2, extent_x + 1, 2, extent_y + 1, 2, channels)
    return folded[
        :,
        tap_z // 2 : tap_z // 2 + extent_z,
        tap_z % 2,
        tap_x // 2 : tap_x // 2 + extent_x,
        tap_x % 2,
        tap_y // 2 : tap_y // 2 + extent_y,
        tap_y % 2,
        :,
    ]


def conv_apply(padded, weight, extent_z, extent_x, extent_y, stride):
    summed = None
    for tap_z in range(3):
        for tap_x in range(3):
            for tap_y in range(3):
                window = tap_window(
                    padded, tap_z, tap_x, tap_y, extent_z, extent_x, extent_y, stride
                )
                flat_tap = window.reshape(-1, window.shape[-1])
                contrib = jnp.dot(
                    flat_tap, weight[tap_z, tap_x, tap_y], preferred_element_type=jnp.float32
                )
                summed = contrib if summed is None else summed + contrib
    return summed.reshape(padded.shape[0], extent_z, extent_x, extent_y, weight.shape[-1])


def kernel_grad(padded, grad_out, extent_z, extent_x, extent_y, stride):
    flat_grad = grad_out.reshape(-1, grad_out.shape[-1])
    results = []
    for tap_z in range(3):
        for tap_x in range(3):
            for tap_y in range(3):
                window = tap_window(
                    padded, tap_z, tap_x, tap_y, extent_z, extent_x, extent_y, stride
                )
                flat_tap = window.reshape(-1, window.shape[-1])
                results.append(
                    lax.dot_general(
                        flat_tap,
                        flat_grad,
                        (((0,), (0,)), ((), ())),
                        preferred_element_type=jnp.float32,
                    )
                )
    return jnp.stack(results).reshape(3, 3, 3, padded.shape[-1], grad_out.shape[-1])


def input_grad(grad_out, weight, extent_z, extent_x, extent_y):
    leading = grad_out.shape[0]
    channels = weight.shape[3]
    flat_grad = grad_out.reshape(-1, grad_out.shape[-1])
    buckets = {}
    for tap_z in range(3):
        for tap_x in range(3):
            for tap_y in range(3):
                contrib = lax.dot_general(
                    flat_grad,
                    weight[tap_z, tap_x, tap_y],
                    (((1,), (1,)), ((), ())),
                    preferred_element_type=jnp.float32,
                )
                contrib = contrib.reshape(leading, extent_z, extent_x, extent_y, channels)
                placed = jnp.pad(
                    contrib,
                    (
                        (0, 0),
                        (tap_z // 2, 1 - tap_z // 2),
                        (tap_x // 2, 1 - tap_x // 2),
                        (tap_y // 2, 1 - tap_y // 2),
                        (0, 0),
                    ),
                )
                parity = (tap_z % 2, tap_x % 2, tap_y % 2)
                buckets[parity] = placed if parity not in buckets else buckets[parity] + placed
    planes_z = []
    for par_z in range(2):
        planes_x = []
        for par_x in range(2):
            planes_x.append(jnp.stack([buckets[par_z, par_x, par_y] for par_y in range(2)], axis=4))
        planes_z.append(jnp.stack(planes_x, axis=3))
    assembled = jnp.stack(planes_z, axis=2)
    assembled = assembled.reshape(
        leading, 2 * extent_z + 2, 2 * extent_x + 2, 2 * extent_y + 2, channels
    )
    return assembled[:, 1:-1, 1:-1, 1:-1, :]


def split_body(volume, targets, front_weight, stride_weight, hidden_weight, output_weight):
    highest = lax.Precision.HIGHEST
    slabs = lax.axis_size("slab")
    batches = lax.axis_size("batch")
    inner = front_weight.shape[-1]
    leading, thick, extent_x, extent_y, channels = volume.shape
    depth = thick * slabs
    outputs = output_weight.shape[-1]
    haloed = with_halo(volume, (("slab", 1),), 1)
    padded = jnp.pad(haloed, ((0, 0), (0, 0), (1, 1), (1, 1), (0, 0)))
    front_pre = conv_apply(padded, front_weight, thick, extent_x, extent_y, 1)
    front_act = jax.nn.silu(front_pre).astype(jnp.bfloat16)
    merged = front_act.reshape(leading, thick, extent_x, extent_y * inner)
    sample_act = lax.all_to_all(merged, "slab", split_axis=0, concat_axis=1, tiled=True)
    sample_act = sample_act.reshape(1, depth, extent_x, extent_y, inner)
    half_z = depth // 2
    half_x = extent_x // 2
    half_y = extent_y // 2
    cells = half_z * half_x * half_y
    stride_pad = jnp.pad(sample_act, ((0, 0), (1, 1), (1, 1), (1, 1), (0, 0)))
    partial_pre = conv_apply(stride_pad, stride_weight, half_z, half_x, half_y, 2)
    stride_pre = lax.psum_scatter(partial_pre, "chan", scatter_dimension=4, tiled=True)
    pooled = jnp.sum(jax.nn.silu(stride_pre), axis=(0, 1, 2, 3)) / cells
    hidden_pre = lax.psum(jnp.dot(pooled, hidden_weight, precision=highest), "chan")
    hidden_act = jax.nn.silu(hidden_pre)
    predicted = jnp.dot(hidden_act, output_weight, precision=highest)
    target_row = lax.dynamic_index_in_dim(targets, lax.axis_index("slab"), 0, keepdims=False)
    residual = predicted - target_row
    squared = jnp.sum(residual * residual)
    grad_output = jnp.outer(hidden_act, residual)
    grad_hidden_pre = jnp.dot(output_weight, residual, precision=highest) * swish_slope(hidden_pre)
    grad_hidden = jnp.outer(pooled, grad_hidden_pre)
    grad_pooled = jnp.dot(hidden_weight, grad_hidden_pre, precision=highest)
    grad_stride_pre = (grad_pooled / cells * swish_slope(stride_pre)).astype(jnp.bfloat16)
    full_grad = lax.all_gather(grad_stride_pre, "chan", axis=4, tiled=True)
    grad_stride = kernel_grad(stride_pad, full_grad, half_z, half_x, half_y, 2)
    grad_act = input_grad(full_grad, stride_weight, half_z, half_x, half_y).astype(jnp.bfloat16)
    returned = lax.all_to_all(
        grad_act.reshape(1, depth, extent_x, extent_y * inner),
        "slab",
        split_axis=1,
        concat_axis=0,
        tiled=True,
    )
    returned = returned.reshape(leading, thick, extent_x, extent_y, inner)
    grad_front_pre = (returned * swish_slope(front_pre)).astype(jnp.bfloat16)
    grad_front = kernel_grad(padded, grad_front_pre, thick, extent_x, extent_y, 1)
    grad_front, grad_stride, grad_hidden, grad_output, squared = lax.psum(
        (grad_front, grad_stride, grad_hidden, grad_output, squared), ("slab", "batch")
    )
    loss = (squared / (slabs * batches * outputs)).reshape(1)
    return (grad_front, grad_stride, grad_hidden, grad_output, loss)


GATHER_LIMIT = 1 << 20


def whole_kernel(
    shape,
    volume_ref, targets_ref, front_turned_ref, stride_ref, hidden_ref, output_ref,
    grad_front_ref, grad_stride_ref, grad_hidden_ref, grad_output_ref, loss_ref,
    taps_ref, front_ref, act_ref, slope_ref, strided_ref, spread_ref, grad_pre_ref,
    front_out_ref, stride_out_ref, front_sem, stride_sem,
):
    slabs, batches, leading, thick, extent_x, extent_y, channels, inner = shape
    f32, bf16 = jnp.float32, jnp.bfloat16
    highest = lax.Precision.HIGHEST
    samples = batches * leading
    depth = slabs * thick
    rows = samples * extent_y
    half_z, half_x, half_y = depth // 2, extent_x // 2, extent_y // 2
    half_rows = samples * half_y
    cells = half_z * half_x * half_y
    wide = 3 * channels
    local_rows = leading * extent_y

    for tap in range(27):
        front_ref[tap] = jnp.transpose(front_turned_ref[tap])

    zeros = jnp.zeros((rows, wide), bf16)
    for x in range(extent_x + 2):
        taps_ref[0, x] = zeros
        taps_ref[depth + 1, x] = zeros

    row = lax.broadcasted_iota(jnp.int32, (rows, channels), 0)
    first = (row & (extent_y - 1)) == 0
    last = (row & (extent_y - 1)) == extent_y - 1
    half_row = lax.broadcasted_iota(jnp.int32, (half_rows, channels), 0)
    half_first = (half_row & (half_y - 1)) == 0
    half_last = (half_row & (half_y - 1)) == half_y - 1

    def fill(slab, carry):
        for plane in range(thick):
            z = slab * thick + plane
            taps_ref[z + 1, 0] = zeros
            taps_ref[z + 1, extent_x + 1] = zeros
            for x in range(extent_x):
                mid = jnp.concatenate(
                    [
                        volume_ref[b * slabs + slab, :, plane, x].astype(f32).reshape(local_rows, channels)
                        for b in range(batches)
                    ],
                    axis=0,
                )
                low = jnp.where(first, 0.0, pltpu.roll(mid, 1, 0))
                high = jnp.where(last, 0.0, pltpu.roll(mid, rows - 1, 0))
                taps_ref[z + 1, x + 1, :, :channels] = low.astype(bf16)
                taps_ref[z + 1, x + 1, :, channels : 2 * channels] = mid.astype(bf16)
                taps_ref[z + 1, x + 1, :, 2 * channels :] = high.astype(bf16)
        return carry

    lax.fori_loop(0, slabs, fill, 0)

    half_zeros = jnp.zeros((half_rows, wide), bf16)
    for x in range(extent_x + 1):
        strided_ref[0, x] = half_zeros

    def front(z, carry):
        total = jnp.zeros((extent_x * rows, channels), f32)
        for kz in range(3):
            for kx in range(3):
                window = taps_ref[z + kz, kx : kx + extent_x].reshape(extent_x * rows, wide)
                kernel = front_ref[3 * (3 * kz + kx) : 3 * (3 * kz + kx) + 3].reshape(wide, channels)
                total += jnp.dot(window, kernel, preferred_element_type=f32)
        logistic = 1.0 / (1.0 + jnp.exp(-total))
        act = (total * logistic).astype(bf16).astype(f32)
        slope = logistic * (1.0 + total * (1.0 - logistic))
        act_ref[z] = act.reshape(extent_x, rows, channels)
        slope_ref[z] = slope.reshape(extent_x, rows, channels)
        strided_ref[z + 1, 0] = half_zeros
        for x in range(extent_x):
            even = act_ref[z, x, pl.ds(0, half_rows, stride=2), :]
            odd = act_ref[z, x, pl.ds(1, half_rows, stride=2), :]
            low = jnp.where(half_first, 0.0, pltpu.roll(odd, 1, 0))
            strided_ref[z + 1, x + 1, :, :channels] = low.astype(bf16)
            strided_ref[z + 1, x + 1, :, channels : 2 * channels] = even.astype(bf16)
            strided_ref[z + 1, x + 1, :, 2 * channels :] = odd.astype(bf16)
        return carry

    lax.fori_loop(0, depth, front, 0)

    def strided_window(kz, kx):
        return jnp.concatenate(
            [strided_ref[kz + 2 * z, kx + 2 * x] for z in range(half_z) for x in range(half_x)], axis=0
        )

    def stride_kernel(kz, kx):
        start = 3 * (3 * kz + kx)
        return stride_ref[start : start + 3].reshape(wide, stride_ref.shape[-1])

    pre = None
    for kz in range(3):
        for kx in range(3):
            term = jnp.dot(strided_window(kz, kx), stride_kernel(kz, kx), preferred_element_type=f32)
            pre = term if pre is None else pre + term
    logistic = 1.0 / (1.0 + jnp.exp(-pre))
    planes = half_z * half_x
    features = pre.shape[-1]
    summed = jnp.sum((pre * logistic).reshape(planes, half_rows, features), axis=0)
    owner = lax.broadcasted_iota(jnp.int32, (samples, half_rows), 1)
    sample = lax.broadcasted_iota(jnp.int32, (samples, half_rows), 0)
    member = ((owner >= sample * half_y) & (owner < (sample + 1) * half_y)).astype(f32)
    pooled = jnp.dot(member, summed, precision=highest, preferred_element_type=f32) / cells
    hidden = hidden_ref[...]
    output = output_ref[...]

    def contract(left, right, dims):
        return lax.dot_general(left, right, (dims, ((), ())), precision=highest, preferred_element_type=f32)

    hidden_pre = contract(pooled, hidden, ((1,), (0,)))
    hidden_logistic = 1.0 / (1.0 + jnp.exp(-hidden_pre))
    hidden_act = hidden_pre * hidden_logistic
    residual = contract(hidden_act, output, ((1,), (1,))) - targets_ref[...]
    loss_ref[...] = jnp.sum(residual * residual, keepdims=True) / (samples * output.shape[0])
    grad_output_ref[...] = contract(residual, hidden_act, ((0,), (0,)))
    hidden_slope = hidden_logistic * (1.0 + hidden_pre * (1.0 - hidden_logistic))
    grad_hidden_pre = contract(residual, output, ((1,), (0,))) * hidden_slope
    share = features // 2
    pooled_own = jnp.where(lax.axis_index("chan") == 0, pooled[:, :share], pooled[:, share:])
    grad_hidden_ref[...] = contract(pooled_own, grad_hidden_pre, ((0,), (0,)))
    grad_pooled = contract(grad_hidden_pre, hidden, ((1,), (1,)))
    grad_rows = contract(member, grad_pooled, ((0,), (0,))) / cells
    slope = logistic * (1.0 + pre * (1.0 - logistic))
    grad_pre = (slope.reshape(planes, half_rows, features) * grad_rows[None]).astype(bf16)
    grad_pre = grad_pre.reshape(planes * half_rows, features)

    def send_out(source, target, sems, group):
        place = pl.ds(3 * group, 3)
        return pltpu.make_async_copy(source.at[place], target.at[place], sems.at[group])

    for kz in range(3):
        for kx in range(3):
            start = 3 * (3 * kz + kx)
            spread = lax.dot_general(
                grad_pre, stride_kernel(kz, kx), (((1,), (1,)), ((), ())), preferred_element_type=f32
            )
            spread_ref[3 * kz + kx] = spread.reshape(planes, half_rows, wide)
            kernel = lax.dot_general(
                strided_window(kz, kx), grad_pre, (((0,), (0,)), ((), ())), preferred_element_type=f32
            )
            for ky in range(3):
                stride_out_ref[start + ky] = kernel[ky * channels : ky * channels + inner]
            send_out(stride_out_ref, grad_stride_ref, stride_sem, 3 * kz + kx).start()

    def sources(cell, half):
        if cell % 2 == 0:
            return [(1, cell // 2)]
        found = [(2, cell // 2)]
        if cell // 2 + 1 < half:
            found.append((0, cell // 2 + 1))
        return found

    for z in range(depth):
        for x in range(extent_x):
            total = None
            for kz, from_z in sources(z, half_z):
                for kx, from_x in sources(x, half_x):
                    block = spread_ref[3 * kz + kx, from_z * half_x + from_x]
                    total = block if total is None else total + block
            even = total[:, channels : 2 * channels]
            up = jnp.where(half_last, 0.0, pltpu.roll(total[:, :channels], half_rows - 1, 0))
            odd = total[:, 2 * channels :] + up
            for start, grad in ((0, even), (1, odd)):
                grad = grad.astype(bf16).astype(f32)
                place = pl.ds(start, half_rows, stride=2)
                grad_pre_ref[z, x, place, :] = grad * slope_ref[z, x, place, :]

    grads = grad_pre_ref[...].reshape(depth * extent_x * rows, channels).astype(bf16)
    grads = jnp.transpose(grads)[:inner]
    for kz in range(3):
        for kx in range(3):
            window = taps_ref[kz : kz + depth, kx : kx + extent_x]
            window = window.reshape(depth * extent_x * rows, wide)
            turned = jnp.dot(grads, window, preferred_element_type=f32)
            for ky in range(3):
                front_out_ref[3 * (3 * kz + kx) + ky] = turned[:, ky * channels : (ky + 1) * channels]
            send_out(front_out_ref, grad_front_ref, front_sem, 3 * kz + kx).start()
    for group in range(9):
        send_out(stride_out_ref, grad_stride_ref, stride_sem, group).wait()
        send_out(front_out_ref, grad_front_ref, front_sem, group).wait()


def whole_batch(shape, features, gathered, targets, front_all, stride_all, hidden_all, output_turned):
    slabs, batches, leading, thick, extent_x, extent_y, channels, inner = shape
    samples, depth = batches * leading, slabs * thick
    rows = samples * extent_y
    half_rows = rows // 2
    planes = depth * extent_x // 4
    f32, bf16 = jnp.float32, jnp.bfloat16
    outputs, hid = output_turned.shape
    vmem = pl.BlockSpec(memory_space=pltpu.VMEM)
    anywhere = pl.BlockSpec(memory_space=pl.ANY)
    return pl.pallas_call(
        functools.partial(whole_kernel, shape),
        out_shape=(
            jax.ShapeDtypeStruct((27, inner, channels), f32),
            jax.ShapeDtypeStruct((27, inner, features), f32),
            jax.ShapeDtypeStruct((features // 2, hid), f32),
            jax.ShapeDtypeStruct((outputs, hid), f32),
            jax.ShapeDtypeStruct((1, 1), f32),
        ),
        in_specs=[vmem] * 6,
        out_specs=[anywhere] * 2 + [vmem] * 3,
        scratch_shapes=[
            pltpu.VMEM((depth + 2, extent_x + 2, rows, 3 * channels), bf16),
            pltpu.VMEM((27, channels, channels), bf16),
            pltpu.VMEM((depth, extent_x, rows, channels), f32),
            pltpu.VMEM((depth, extent_x, rows, channels), f32),
            pltpu.VMEM((depth + 1, extent_x + 1, half_rows, 3 * channels), bf16),
            pltpu.VMEM((9, planes, half_rows, 3 * channels), f32),
            pltpu.VMEM((depth, extent_x, rows, channels), f32),
            pltpu.VMEM((27, inner, channels), f32),
            pltpu.VMEM((27, inner, features), f32),
            pltpu.SemaphoreType.DMA((9,)),
            pltpu.SemaphoreType.DMA((9,)),
        ],
        compiler_params=pltpu.CompilerParams(vmem_limit_bytes=40 << 20),
    )(gathered, targets, front_all, stride_all, hidden_all, output_turned)


def gather_kernel(
    slabs, batches,
    volume_ref, targets_ref, front_ref, stride_ref, hidden_ref,
    gathered_ref, targets_all_ref, front_all_ref, stride_all_ref, hidden_all_ref,
    local_sem, slab_sem, batch_sem, piece_sem, pair_send_sem, pair_sem,
    target_send_sem, target_sem, weight_send_sem, weight_sem,
):
    slab, batch, chan = lax.axis_index("slab"), lax.axis_index("batch"), lax.axis_index("chan")
    sibling = {"chan": 1 - chan}
    half = volume_ref.shape[0] // 2
    inner = front_ref.shape[1]
    share = hidden_ref.shape[0]

    def remote(source, target, send_sem, recv_sem, device):
        return pltpu.make_async_remote_copy(
            src_ref=source, dst_ref=target, send_sem=send_sem, recv_sem=recv_sem,
            device_id=device, device_id_type=pl.DeviceIdType.MESH,
        )

    slab_steps = range(1, slabs)
    batch_steps = range(1, batches)
    to_slab = [{"slab": lax.rem(slab + step, slabs)} for step in slab_steps]
    to_batch = [{"batch": lax.rem(batch + step, batches)} for step in batch_steps]
    from_slab = [lax.rem(slab + slabs - step, slabs) for step in slab_steps]
    from_batch = [lax.rem(batch + batches - step, batches) for step in batch_steps]

    barrier = pltpu.get_barrier_semaphore()
    neighbours = to_slab + to_batch + [sibling]
    for device in neighbours:
        pl.semaphore_signal(barrier, inc=1, device_id=device, device_id_type=pl.DeviceIdType.MESH)
    pl.semaphore_wait(barrier, len(neighbours))

    def part(piece, side):
        return gathered_ref.at[piece, pl.ds(side * half, half)]

    mine = batch * slabs + slab
    own = volume_ref.at[pl.ds(chan * half, half)]
    sends = []

    def send(copy):
        copy.start()
        sends.append(copy)

    for i, device in enumerate(to_slab):
        send(remote(own, part(mine, chan), slab_sem.at[i], piece_sem.at[mine], device))
    for i, device in enumerate(to_batch):
        send(remote(own, part(mine, chan), batch_sem.at[0, i], piece_sem.at[mine], device))
        send(remote(targets_ref, targets_all_ref.at[batch], target_send_sem.at[i], target_sem.at[batch], device))
    weights = [
        remote(front_ref, front_all_ref.at[:, pl.ds(inner, inner)], weight_send_sem.at[0], weight_sem.at[0], sibling),
        remote(stride_ref, stride_all_ref.at[:, pl.ds(inner, inner)], weight_send_sem.at[1], weight_sem.at[1], sibling),
        remote(hidden_ref, hidden_all_ref.at[pl.ds(chan * share, share)], weight_send_sem.at[2], weight_sem.at[2], sibling),
    ]
    for copy in weights:
        send(copy)
    local = [
        pltpu.make_async_copy(volume_ref, gathered_ref.at[mine], local_sem.at[0]),
        pltpu.make_async_copy(targets_ref, targets_all_ref.at[batch], local_sem.at[1]),
        pltpu.make_async_copy(front_ref, front_all_ref.at[:, pl.ds(0, inner)], local_sem.at[2]),
        pltpu.make_async_copy(stride_ref, stride_all_ref.at[:, pl.ds(0, inner)], local_sem.at[3]),
        pltpu.make_async_copy(hidden_ref, hidden_all_ref.at[pl.ds(chan * share, share)], local_sem.at[4]),
    ]
    for copy in local:
        copy.start()

    def arrived(piece, side, sem, device):
        remote(part(piece, side), part(piece, side), slab_sem.at[0], sem.at[piece], device).wait_recv()

    def pass_on(slot, piece):
        send(remote(part(piece, chan), part(piece, chan), pair_send_sem.at[slot], pair_sem.at[piece], sibling))

    slot = 0
    for j, source in enumerate(from_slab):
        piece = batch * slabs + source
        arrived(piece, chan, piece_sem, sibling)
        for i, device in enumerate(to_batch):
            send(remote(part(piece, chan), part(piece, chan), batch_sem.at[j + 1, i], piece_sem.at[piece], device))
        pass_on(slot, piece)
        slot += 1
    for source in from_batch:
        for slab_source in [slab] + from_slab:
            piece = source * slabs + slab_source
            arrived(piece, chan, piece_sem, sibling)
            pass_on(slot, piece)
            slot += 1
        remote(
            targets_ref, targets_all_ref.at[source], target_send_sem.at[0], target_sem.at[source], sibling
        ).wait_recv()
    for source in [batch] + from_batch:
        for slab_source in [slab] + from_slab:
            if source is batch and slab_source is slab:
                continue
            arrived(source * slabs + slab_source, 1 - chan, pair_sem, sibling)
    for copy in weights:
        copy.wait_recv()
    for copy in local:
        copy.wait()
    for copy in sends:
        copy.wait_send()


def gather_inputs(volume, targets, front_turned, stride_own, hidden_weight):
    slabs, batches = lax.axis_size("slab"), lax.axis_size("batch")
    pieces = slabs * batches
    vmem = pl.BlockSpec(memory_space=pltpu.VMEM)
    hbm = pl.BlockSpec(memory_space=pltpu.HBM)
    taps, inner, channels = front_turned.shape
    features = stride_own.shape[-1]
    share, hid = hidden_weight.shape
    dma = pltpu.SemaphoreType.DMA
    return pl.pallas_call(
        functools.partial(gather_kernel, slabs, batches),
        out_shape=(
            jax.ShapeDtypeStruct((pieces,) + volume.shape, volume.dtype),
            jax.ShapeDtypeStruct((batches,) + targets.shape, targets.dtype),
            jax.ShapeDtypeStruct((taps, 2 * inner, channels), front_turned.dtype),
            jax.ShapeDtypeStruct((taps, 2 * inner, features), stride_own.dtype),
            jax.ShapeDtypeStruct((2 * share, hid), hidden_weight.dtype),
        ),
        in_specs=[hbm] * 5,
        out_specs=[vmem] * 5,
        scratch_shapes=[
            dma((5,)), dma((slabs,)), dma((slabs, batches)), dma((pieces,)), dma((pieces,)), dma((pieces,)),
            dma((batches,)), dma((batches,)), dma((3,)), dma((3,)),
        ],
        compiler_params=pltpu.CompilerParams(
            collective_id=0, has_side_effects=True, vmem_limit_bytes=16 << 20
        ),
    )(volume, targets, front_turned, stride_own, hidden_weight)


def body(volume, targets, front_weight, stride_weight, hidden_weight, output_weight):
    slabs = lax.axis_size("slab")
    batches = lax.axis_size("batch")
    if volume.size * 2 * slabs * batches > GATHER_LIMIT or volume.shape[0] % 2:
        return split_body(volume, targets, front_weight, stride_weight, hidden_weight, output_weight)
    inner = front_weight.shape[-1]
    channels = volume.shape[-1]
    features = stride_weight.shape[-1]
    shape = (slabs, batches) + volume.shape + (inner,)
    front_turned = jnp.swapaxes(front_weight.reshape(27, channels, inner), 1, 2)
    stride_own = stride_weight.reshape(27, inner, features)
    gathered, targets, front_all, stride_all, hidden_all = gather_inputs(
        volume, targets, front_turned, stride_own, hidden_weight
    )
    grad_front, grad_stride, grad_hidden, grad_output, loss = whole_batch(
        shape, features, gathered, targets.reshape(-1, targets.shape[-1]),
        front_all, stride_all, hidden_all, output_weight.T,
    )
    return (
        jnp.swapaxes(grad_front, 1, 2).reshape(3, 3, 3, channels, inner),
        grad_stride.reshape(3, 3, 3, inner, features),
        grad_hidden,
        grad_output.T,
        loss.reshape(1),
    )


def solution(mesh):
    in_specs = (
        P(("groups", "batch"), "slab", None, None, None),
        P(("groups", "batch"), None),
        P(None, None, None, None, "chan"),
        P(None, None, None, "chan", None),
        P("chan", None),
        P(),
    )
    out_specs = (
        P("groups", None, None, None, "chan"),
        P("groups", None, None, "chan", None),
        P(("groups", "chan"), None),
        P("groups", None),
        P("groups"),
    )
    return jax.shard_map(body, mesh=mesh, in_specs=in_specs, out_specs=out_specs, check_vma=False)
```

```python
import functools

import jax
import jax.numpy as jnp
from jax import lax
from jax.experimental import pallas as pl
from jax.experimental.pallas import tpu as pltpu
from jax.sharding import PartitionSpec as P


def with_halo(cells, sides, width):
    for axis, dim in sides:
        count = lax.axis_size(axis)
        ends = count - 1
        head = lax.slice_in_dim(cells, 0, width, axis=dim)
        tail = lax.slice_in_dim(cells, cells.shape[dim] - width, cells.shape[dim], axis=dim)
        cells = jnp.concatenate(
            [
                lax.ppermute(tail, axis, [(i, (i + 1) % count) for i in range(ends)]),
                cells,
                lax.ppermute(head, axis, [((i + 1) % count, i) for i in range(ends)]),
            ],
            axis=dim,
        )
    return cells


def swish_slope(preact):
    logistic = jax.nn.sigmoid(preact)
    return logistic * (1.0 + preact * (1.0 - logistic))


def tap_window(padded, tap_z, tap_x, tap_y, extent_z, extent_x, extent_y, stride):
    if stride == 1:
        return padded[
            :, tap_z : tap_z + extent_z, tap_x : tap_x + extent_x, tap_y : tap_y + extent_y, :
        ]
    leading = padded.shape[0]
    channels = padded.shape[-1]
    folded = padded.reshape(leading, extent_z + 1, 2, extent_x + 1, 2, extent_y + 1, 2, channels)
    return folded[
        :,
        tap_z // 2 : tap_z // 2 + extent_z,
        tap_z % 2,
        tap_x // 2 : tap_x // 2 + extent_x,
        tap_x % 2,
        tap_y // 2 : tap_y // 2 + extent_y,
        tap_y % 2,
        :,
    ]


def conv_apply(padded, weight, extent_z, extent_x, extent_y, stride):
    summed = None
    for tap_z in range(3):
        for tap_x in range(3):
            for tap_y in range(3):
                window = tap_window(
                    padded, tap_z, tap_x, tap_y, extent_z, extent_x, extent_y, stride
                )
                flat_tap = window.reshape(-1, window.shape[-1])
                contrib = jnp.dot(
                    flat_tap, weight[tap_z, tap_x, tap_y], preferred_element_type=jnp.float32
                )
                summed = contrib if summed is None else summed + contrib
    return summed.reshape(padded.shape[0], extent_z, extent_x, extent_y, weight.shape[-1])


def kernel_grad(padded, grad_out, extent_z, extent_x, extent_y, stride):
    flat_grad = grad_out.reshape(-1, grad_out.shape[-1])
    results = []
    for tap_z in range(3):
        for tap_x in range(3):
            for tap_y in range(3):
                window = tap_window(
                    padded, tap_z, tap_x, tap_y, extent_z, extent_x, extent_y, stride
                )
                flat_tap = window.reshape(-1, window.shape[-1])
                results.append(
                    lax.dot_general(
                        flat_tap,
                        flat_grad,
                        (((0,), (0,)), ((), ())),
                        preferred_element_type=jnp.float32,
                    )
                )
    return jnp.stack(results).reshape(3, 3, 3, padded.shape[-1], grad_out.shape[-1])


def input_grad(grad_out, weight, extent_z, extent_x, extent_y):
    leading = grad_out.shape[0]
    channels = weight.shape[3]
    flat_grad = grad_out.reshape(-1, grad_out.shape[-1])
    buckets = {}
    for tap_z in range(3):
        for tap_x in range(3):
            for tap_y in range(3):
                contrib = lax.dot_general(
                    flat_grad,
                    weight[tap_z, tap_x, tap_y],
                    (((1,), (1,)), ((), ())),
                    preferred_element_type=jnp.float32,
                )
                contrib = contrib.reshape(leading, extent_z, extent_x, extent_y, channels)
                placed = jnp.pad(
                    contrib,
                    (
                        (0, 0),
                        (tap_z // 2, 1 - tap_z // 2),
                        (tap_x // 2, 1 - tap_x // 2),
                        (tap_y // 2, 1 - tap_y // 2),
                        (0, 0),
                    ),
                )
                parity = (tap_z % 2, tap_x % 2, tap_y % 2)
                buckets[parity] = placed if parity not in buckets else buckets[parity] + placed
    planes_z = []
    for par_z in range(2):
        planes_x = []
        for par_x in range(2):
            planes_x.append(jnp.stack([buckets[par_z, par_x, par_y] for par_y in range(2)], axis=4))
        planes_z.append(jnp.stack(planes_x, axis=3))
    assembled = jnp.stack(planes_z, axis=2)
    assembled = assembled.reshape(
        leading, 2 * extent_z + 2, 2 * extent_x + 2, 2 * extent_y + 2, channels
    )
    return assembled[:, 1:-1, 1:-1, 1:-1, :]


def split_body(volume, targets, front_weight, stride_weight, hidden_weight, output_weight):
    highest = lax.Precision.HIGHEST
    slabs = lax.axis_size("slab")
    batches = lax.axis_size("batch")
    inner = front_weight.shape[-1]
    leading, thick, extent_x, extent_y, channels = volume.shape
    depth = thick * slabs
    outputs = output_weight.shape[-1]
    haloed = with_halo(volume, (("slab", 1),), 1)
    padded = jnp.pad(haloed, ((0, 0), (0, 0), (1, 1), (1, 1), (0, 0)))
    front_pre = conv_apply(padded, front_weight, thick, extent_x, extent_y, 1)
    front_act = jax.nn.silu(front_pre).astype(jnp.bfloat16)
    merged = front_act.reshape(leading, thick, extent_x, extent_y * inner)
    sample_act = lax.all_to_all(merged, "slab", split_axis=0, concat_axis=1, tiled=True)
    sample_act = sample_act.reshape(1, depth, extent_x, extent_y, inner)
    half_z = depth // 2
    half_x = extent_x // 2
    half_y = extent_y // 2
    cells = half_z * half_x * half_y
    stride_pad = jnp.pad(sample_act, ((0, 0), (1, 1), (1, 1), (1, 1), (0, 0)))
    partial_pre = conv_apply(stride_pad, stride_weight, half_z, half_x, half_y, 2)
    stride_pre = lax.psum_scatter(partial_pre, "chan", scatter_dimension=4, tiled=True)
    pooled = jnp.sum(jax.nn.silu(stride_pre), axis=(0, 1, 2, 3)) / cells
    hidden_pre = lax.psum(jnp.dot(pooled, hidden_weight, precision=highest), "chan")
    hidden_act = jax.nn.silu(hidden_pre)
    predicted = jnp.dot(hidden_act, output_weight, precision=highest)
    target_row = lax.dynamic_index_in_dim(targets, lax.axis_index("slab"), 0, keepdims=False)
    residual = predicted - target_row
    squared = jnp.sum(residual * residual)
    grad_output = jnp.outer(hidden_act, residual)
    grad_hidden_pre = jnp.dot(output_weight, residual, precision=highest) * swish_slope(hidden_pre)
    grad_hidden = jnp.outer(pooled, grad_hidden_pre)
    grad_pooled = jnp.dot(hidden_weight, grad_hidden_pre, precision=highest)
    grad_stride_pre = (grad_pooled / cells * swish_slope(stride_pre)).astype(jnp.bfloat16)
    full_grad = lax.all_gather(grad_stride_pre, "chan", axis=4, tiled=True)
    grad_stride = kernel_grad(stride_pad, full_grad, half_z, half_x, half_y, 2)
    grad_act = input_grad(full_grad, stride_weight, half_z, half_x, half_y).astype(jnp.bfloat16)
    returned = lax.all_to_all(
        grad_act.reshape(1, depth, extent_x, extent_y * inner),
        "slab",
        split_axis=1,
        concat_axis=0,
        tiled=True,
    )
    returned = returned.reshape(leading, thick, extent_x, extent_y, inner)
    grad_front_pre = (returned * swish_slope(front_pre)).astype(jnp.bfloat16)
    grad_front = kernel_grad(padded, grad_front_pre, thick, extent_x, extent_y, 1)
    grad_front, grad_stride, grad_hidden, grad_output, squared = lax.psum(
        (grad_front, grad_stride, grad_hidden, grad_output, squared), ("slab", "batch")
    )
    loss = (squared / (slabs * batches * outputs)).reshape(1)
    return (grad_front, grad_stride, grad_hidden, grad_output, loss)


GATHER_LIMIT = 1 << 20


def whole_kernel(
    shape,
    gathered_hbm, targets_hbm, front_own_hbm, front_other_hbm, stride_own_hbm, stride_other_hbm,
    hidden_hbm, output_hbm,
    grad_front_ref, grad_stride_ref, grad_hidden_ref, grad_output_ref, loss_ref,
    taps_ref, front_ref, act_ref, slope_ref, strided_ref, spread_ref, grad_pre_ref,
    front_out_ref, stride_out_ref, front_sem, stride_sem,
    volume_ref, targets_ref, front_turned_ref, stride_ref, hidden_ref, output_ref, front_pre_ref, fetch_sem,
):
    slabs, batches, leading, thick, extent_x, extent_y, channels, inner = shape
    f32, bf16 = jnp.float32, jnp.bfloat16
    highest = lax.Precision.HIGHEST
    samples = batches * leading
    depth = slabs * thick
    rows = samples * extent_y
    half_z, half_x, half_y = depth // 2, extent_x // 2, extent_y // 2
    half_rows = samples * half_y
    cells = half_z * half_x * half_y
    wide = 3 * channels
    local_rows = leading * extent_y

    fetches = [
        pltpu.make_async_copy(source, target, fetch_sem.at[i])
        for i, (source, target) in enumerate(
            [
                (gathered_hbm, volume_ref),
                (front_own_hbm, front_turned_ref.at[:, pl.ds(0, inner)]),
                (front_other_hbm, front_turned_ref.at[:, pl.ds(inner, inner)]),
                (stride_own_hbm, stride_ref.at[:, pl.ds(0, inner)]),
                (stride_other_hbm, stride_ref.at[:, pl.ds(inner, inner)]),
                (hidden_hbm, hidden_ref),
                (output_hbm, output_ref),
                (targets_hbm, targets_ref),
            ]
        )
    ]
    for fetch in fetches:
        fetch.start()

    zeros = jnp.zeros((rows, wide), bf16)
    for x in range(extent_x + 2):
        taps_ref[0, x] = zeros
        taps_ref[depth + 1, x] = zeros

    row = lax.broadcasted_iota(jnp.int32, (rows, channels), 0)
    first = (row & (extent_y - 1)) == 0
    last = (row & (extent_y - 1)) == extent_y - 1
    half_row = lax.broadcasted_iota(jnp.int32, (half_rows, channels), 0)
    half_first = (half_row & (half_y - 1)) == 0
    half_last = (half_row & (half_y - 1)) == half_y - 1

    def fill(slab, carry):
        for plane in range(thick):
            z = slab * thick + plane
            taps_ref[z + 1, 0] = zeros
            taps_ref[z + 1, extent_x + 1] = zeros
            for x in range(extent_x):
                mid = jnp.concatenate(
                    [
                        volume_ref[b * slabs + slab, :, plane, x].astype(f32).reshape(local_rows, channels)
                        for b in range(batches)
                    ],
                    axis=0,
                )
                low = jnp.where(first, 0.0, pltpu.roll(mid, 1, 0))
                high = jnp.where(last, 0.0, pltpu.roll(mid, rows - 1, 0))
                taps_ref[z + 1, x + 1, :, :channels] = low.astype(bf16)
                taps_ref[z + 1, x + 1, :, channels : 2 * channels] = mid.astype(bf16)
                taps_ref[z + 1, x + 1, :, 2 * channels :] = high.astype(bf16)
        return carry

    half_zeros = jnp.zeros((half_rows, wide), bf16)
    for x in range(extent_x + 1):
        strided_ref[0, x] = half_zeros
    front_pre_ref[1] = jnp.zeros((extent_x * rows, channels), f32)
    fetches[0].wait()
    lax.fori_loop(0, slabs, fill, 0)
    fetches[1].wait()
    fetches[2].wait()
    for kz in range(3):
        for tap in range(9):
            front_ref[tap * channels : (tap + 1) * channels, kz * channels : (kz + 1) * channels] = jnp.transpose(
                front_turned_ref[9 * kz + tap]
            )

    def front_taps(z, carry):
        window = jnp.concatenate(
            [taps_ref[z + 1, kx : kx + extent_x].reshape(extent_x * rows, wide) for kx in range(3)], axis=1
        )
        spread = jnp.dot(window, front_ref[...], preferred_element_type=f32)
        front_pre_ref[z + 2] = spread[:, :channels]
        front_pre_ref[z + 1] += spread[:, channels : 2 * channels]

        @pl.when(z > 0)
        def _():
            front_pre_ref[z] += spread[:, 2 * channels :]

        return carry

    lax.fori_loop(0, depth, front_taps, 0)

    def front(z, carry):
        total = front_pre_ref[z + 1]
        logistic = 1.0 / (1.0 + jnp.exp(-total))
        act = (total * logistic).astype(bf16).astype(f32)
        slope = logistic * (1.0 + total * (1.0 - logistic))
        act_ref[z] = act.reshape(extent_x, rows, channels)
        slope_ref[z] = slope.reshape(extent_x, rows, channels)
        strided_ref[z + 1, 0] = half_zeros
        for x in range(extent_x):
            even = act_ref[z, x, pl.ds(0, half_rows, stride=2), :]
            odd = act_ref[z, x, pl.ds(1, half_rows, stride=2), :]
            low = jnp.where(half_first, 0.0, pltpu.roll(odd, 1, 0))
            strided_ref[z + 1, x + 1, :, :channels] = low.astype(bf16)
            strided_ref[z + 1, x + 1, :, channels : 2 * channels] = even.astype(bf16)
            strided_ref[z + 1, x + 1, :, 2 * channels :] = odd.astype(bf16)
        return carry

    lax.fori_loop(0, depth, front, 0)

    def strided_window(kz, kx):
        return jnp.concatenate(
            [strided_ref[kz + 2 * z, kx + 2 * x] for z in range(half_z) for x in range(half_x)], axis=0
        )

    def stride_kernel(kz, kx):
        start = 3 * (3 * kz + kx)
        return stride_ref[start : start + 3].reshape(wide, stride_ref.shape[-1])

    for fetch in fetches[3:]:
        fetch.wait()
    windows = jnp.concatenate([strided_window(kz, kx) for kz in range(3) for kx in range(3)], axis=1)
    pre = jnp.dot(windows, stride_ref[...].reshape(27 * channels, stride_ref.shape[-1]), preferred_element_type=f32)
    logistic = 1.0 / (1.0 + jnp.exp(-pre))
    planes = half_z * half_x
    features = pre.shape[-1]
    summed = jnp.sum((pre * logistic).reshape(planes, half_rows, features), axis=0)
    owner = lax.broadcasted_iota(jnp.int32, (samples, half_rows), 1)
    sample = lax.broadcasted_iota(jnp.int32, (samples, half_rows), 0)
    member = ((owner >= sample * half_y) & (owner < (sample + 1) * half_y)).astype(f32)
    pooled = jnp.dot(member, summed, precision=highest, preferred_element_type=f32) / cells
    hidden = hidden_ref[...]
    output = output_ref[...]

    def contract(left, right, dims):
        return lax.dot_general(left, right, (dims, ((), ())), precision=highest, preferred_element_type=f32)

    hidden_pre = contract(pooled, hidden, ((1,), (0,)))
    hidden_logistic = 1.0 / (1.0 + jnp.exp(-hidden_pre))
    hidden_act = hidden_pre * hidden_logistic
    residual = contract(hidden_act, output, ((1,), (1,))) - targets_ref[...]
    loss_ref[...] = jnp.sum(residual * residual, keepdims=True) / (samples * output.shape[0])
    grad_output_ref[...] = contract(residual, hidden_act, ((0,), (0,)))
    hidden_slope = hidden_logistic * (1.0 + hidden_pre * (1.0 - hidden_logistic))
    grad_hidden_pre = contract(residual, output, ((1,), (0,))) * hidden_slope
    share = features // 2
    pooled_own = jnp.where(lax.axis_index("chan") == 0, pooled[:, :share], pooled[:, share:])
    grad_hidden_ref[...] = contract(pooled_own, grad_hidden_pre, ((0,), (0,)))
    grad_pooled = contract(grad_hidden_pre, hidden, ((1,), (1,)))
    grad_rows = contract(member, grad_pooled, ((0,), (0,))) / cells
    slope = logistic * (1.0 + pre * (1.0 - logistic))
    grad_pre = (slope.reshape(planes, half_rows, features) * grad_rows[None]).astype(bf16)
    grad_pre = grad_pre.reshape(planes * half_rows, features)

    def send_out(source, target, sems, group):
        place = pl.ds(3 * group, 3)
        return pltpu.make_async_copy(source.at[place], target.at[place], sems.at[group])

    for kz in range(3):
        for kx in range(3):
            start = 3 * (3 * kz + kx)
            spread = lax.dot_general(
                grad_pre, stride_kernel(kz, kx), (((1,), (1,)), ((), ())), preferred_element_type=f32
            )
            spread_ref[3 * kz + kx] = spread.reshape(planes, half_rows, wide)
            kernel = lax.dot_general(
                strided_window(kz, kx), grad_pre, (((0,), (0,)), ((), ())), preferred_element_type=f32
            )
            for ky in range(3):
                stride_out_ref[start + ky] = kernel[ky * channels : ky * channels + inner]
            send_out(stride_out_ref, grad_stride_ref, stride_sem, 3 * kz + kx).start()

    def sources(cell, half):
        if cell % 2 == 0:
            return [(1, cell // 2)]
        found = [(2, cell // 2)]
        if cell // 2 + 1 < half:
            found.append((0, cell // 2 + 1))
        return found

    for z in range(depth):
        for x in range(extent_x):
            total = None
            for kz, from_z in sources(z, half_z):
                for kx, from_x in sources(x, half_x):
                    block = spread_ref[3 * kz + kx, from_z * half_x + from_x]
                    total = block if total is None else total + block
            even = total[:, channels : 2 * channels]
            up = jnp.where(half_last, 0.0, pltpu.roll(total[:, :channels], half_rows - 1, 0))
            odd = total[:, 2 * channels :] + up
            for start, grad in ((0, even), (1, odd)):
                grad = grad.astype(bf16).astype(f32)
                place = pl.ds(start, half_rows, stride=2)
                grad_pre_ref[z, x, place, :] = grad * slope_ref[z, x, place, :]

    grads = grad_pre_ref[...].reshape(depth * extent_x * rows, channels).astype(bf16)
    grads = jnp.transpose(grads)[:inner]
    for kz in range(3):
        for kx in range(3):
            window = taps_ref[kz : kz + depth, kx : kx + extent_x]
            window = window.reshape(depth * extent_x * rows, wide)
            turned = jnp.dot(grads, window, preferred_element_type=f32)
            for ky in range(3):
                front_out_ref[3 * (3 * kz + kx) + ky] = turned[:, ky * channels : (ky + 1) * channels]
            send_out(front_out_ref, grad_front_ref, front_sem, 3 * kz + kx).start()
    for group in range(9):
        send_out(stride_out_ref, grad_stride_ref, stride_sem, group).wait()
        send_out(front_out_ref, grad_front_ref, front_sem, group).wait()


def whole_batch(shape, features, gathered, targets, front_own, front_other, stride_own, stride_other, hidden_all, output_turned):
    slabs, batches, leading, thick, extent_x, extent_y, channels, inner = shape
    samples, depth = batches * leading, slabs * thick
    rows = samples * extent_y
    half_rows = rows // 2
    planes = depth * extent_x // 4
    f32, bf16 = jnp.float32, jnp.bfloat16
    outputs, hid = output_turned.shape
    vmem = pl.BlockSpec(memory_space=pltpu.VMEM)
    anywhere = pl.BlockSpec(memory_space=pl.ANY)
    return pl.pallas_call(
        functools.partial(whole_kernel, shape),
        out_shape=(
            jax.ShapeDtypeStruct((27, inner, channels), f32),
            jax.ShapeDtypeStruct((27, inner, features), f32),
            jax.ShapeDtypeStruct((features // 2, hid), f32),
            jax.ShapeDtypeStruct((outputs, hid), f32),
            jax.ShapeDtypeStruct((1, 1), f32),
        ),
        in_specs=[anywhere] * 8,
        out_specs=[anywhere] * 2 + [vmem] * 3,
        scratch_shapes=[
            pltpu.VMEM((depth + 2, extent_x + 2, rows, 3 * channels), bf16),
            pltpu.VMEM((9 * channels, 3 * channels), bf16),
            pltpu.VMEM((depth, extent_x, rows, channels), f32),
            pltpu.VMEM((depth, extent_x, rows, channels), f32),
            pltpu.VMEM((depth + 1, extent_x + 1, half_rows, 3 * channels), bf16),
            pltpu.VMEM((9, planes, half_rows, 3 * channels), f32),
            pltpu.VMEM((depth, extent_x, rows, channels), f32),
            pltpu.VMEM((27, inner, channels), f32),
            pltpu.VMEM((27, inner, features), f32),
            pltpu.SemaphoreType.DMA((9,)),
            pltpu.SemaphoreType.DMA((9,)),
            pltpu.VMEM(gathered.shape, bf16),
            pltpu.VMEM(targets.shape, f32),
            pltpu.VMEM((27, channels, channels), bf16),
            pltpu.VMEM((27, channels, features), bf16),
            pltpu.VMEM(hidden_all.shape, f32),
            pltpu.VMEM(output_turned.shape, f32),
            pltpu.VMEM((depth + 2, extent_x * rows, channels), f32),
            pltpu.SemaphoreType.DMA((8,)),
        ],
        compiler_params=pltpu.CompilerParams(vmem_limit_bytes=60 << 20),
    )(gathered, targets, front_own, front_other, stride_own, stride_other, hidden_all, output_turned)


def gather_kernel(
    slabs, batches,
    volume_ref, targets_ref, front_ref, stride_ref, hidden_ref,
    gathered_ref, targets_all_ref, front_other_ref, stride_other_ref, hidden_all_ref,
    local_sem, slab_sem, batch_sem, piece_sem, pair_send_sem, pair_sem,
    target_send_sem, target_sem, weight_send_sem, weight_sem,
):
    slab, batch, chan = lax.axis_index("slab"), lax.axis_index("batch"), lax.axis_index("chan")
    sibling = {"chan": 1 - chan}
    half = volume_ref.shape[0] // 2
    share = hidden_ref.shape[0]

    def remote(source, target, send_sem, recv_sem, device):
        return pltpu.make_async_remote_copy(
            src_ref=source, dst_ref=target, send_sem=send_sem, recv_sem=recv_sem,
            device_id=device, device_id_type=pl.DeviceIdType.MESH,
        )

    slab_steps = range(1, slabs)
    batch_steps = range(1, batches)
    to_slab = [{"slab": lax.rem(slab + step, slabs)} for step in slab_steps]
    to_batch = [{"batch": lax.rem(batch + step, batches)} for step in batch_steps]
    from_slab = [lax.rem(slab + slabs - step, slabs) for step in slab_steps]
    from_batch = [lax.rem(batch + batches - step, batches) for step in batch_steps]

    barrier = pltpu.get_barrier_semaphore()
    neighbours = to_slab + to_batch + [sibling]
    for device in neighbours:
        pl.semaphore_signal(barrier, inc=1, device_id=device, device_id_type=pl.DeviceIdType.MESH)
    pl.semaphore_wait(barrier, len(neighbours))

    def part(piece, side):
        return gathered_ref.at[piece, pl.ds(side * half, half)]

    mine = batch * slabs + slab
    own = volume_ref.at[pl.ds(chan * half, half)]
    sends = []

    def send(copy):
        copy.start()
        sends.append(copy)

    for i, device in enumerate(to_slab):
        send(remote(own, part(mine, chan), slab_sem.at[i], piece_sem.at[mine], device))
    for i, device in enumerate(to_batch):
        send(remote(own, part(mine, chan), batch_sem.at[0, i], piece_sem.at[mine], device))
        send(remote(targets_ref, targets_all_ref.at[batch], target_send_sem.at[i], target_sem.at[batch], device))
    weights = [
        remote(front_ref, front_other_ref, weight_send_sem.at[0], weight_sem.at[0], sibling),
        remote(stride_ref, stride_other_ref, weight_send_sem.at[1], weight_sem.at[1], sibling),
        remote(hidden_ref, hidden_all_ref.at[pl.ds(chan * share, share)], weight_send_sem.at[2], weight_sem.at[2], sibling),
    ]
    for copy in weights:
        send(copy)
    local = [
        pltpu.make_async_copy(volume_ref, gathered_ref.at[mine], local_sem.at[0]),
        pltpu.make_async_copy(targets_ref, targets_all_ref.at[batch], local_sem.at[1]),
        pltpu.make_async_copy(hidden_ref, hidden_all_ref.at[pl.ds(chan * share, share)], local_sem.at[2]),
    ]
    for copy in local:
        copy.start()

    def arrived(piece, side, sem, device):
        remote(part(piece, side), part(piece, side), slab_sem.at[0], sem.at[piece], device).wait_recv()

    def pass_on(slot, piece):
        send(remote(part(piece, chan), part(piece, chan), pair_send_sem.at[slot], pair_sem.at[piece], sibling))

    slot = 0
    for j, source in enumerate(from_slab):
        piece = batch * slabs + source
        arrived(piece, chan, piece_sem, sibling)
        for i, device in enumerate(to_batch):
            send(remote(part(piece, chan), part(piece, chan), batch_sem.at[j + 1, i], piece_sem.at[piece], device))
        pass_on(slot, piece)
        slot += 1
    for source in from_batch:
        for slab_source in [slab] + from_slab:
            piece = source * slabs + slab_source
            arrived(piece, chan, piece_sem, sibling)
            pass_on(slot, piece)
            slot += 1
        remote(
            targets_ref, targets_all_ref.at[source], target_send_sem.at[0], target_sem.at[source], sibling
        ).wait_recv()
    for source in [batch] + from_batch:
        for slab_source in [slab] + from_slab:
            if source is batch and slab_source is slab:
                continue
            arrived(source * slabs + slab_source, 1 - chan, pair_sem, sibling)
    for copy in weights:
        copy.wait_recv()
    for copy in local:
        copy.wait()
    for copy in sends:
        copy.wait_send()


def gather_inputs(volume, targets, front_turned, stride_own, hidden_weight):
    slabs, batches = lax.axis_size("slab"), lax.axis_size("batch")
    pieces = slabs * batches
    anywhere = pl.BlockSpec(memory_space=pl.ANY)
    share, hid = hidden_weight.shape
    dma = pltpu.SemaphoreType.DMA
    return pl.pallas_call(
        functools.partial(gather_kernel, slabs, batches),
        out_shape=(
            jax.ShapeDtypeStruct((pieces,) + volume.shape, volume.dtype),
            jax.ShapeDtypeStruct((batches,) + targets.shape, targets.dtype),
            jax.ShapeDtypeStruct(front_turned.shape, front_turned.dtype),
            jax.ShapeDtypeStruct(stride_own.shape, stride_own.dtype),
            jax.ShapeDtypeStruct((2 * share, hid), hidden_weight.dtype),
        ),
        in_specs=[anywhere] * 5,
        out_specs=[anywhere] * 5,
        scratch_shapes=[
            dma((3,)), dma((slabs,)), dma((slabs, batches)), dma((pieces,)), dma((pieces,)), dma((pieces,)),
            dma((batches,)), dma((batches,)), dma((3,)), dma((3,)),
        ],
        compiler_params=pltpu.CompilerParams(
            collective_id=0, has_side_effects=True, vmem_limit_bytes=60 << 20
        ),
    )(volume, targets, front_turned, stride_own, hidden_weight)


def body(volume, targets, front_weight, stride_weight, hidden_weight, output_weight):
    slabs = lax.axis_size("slab")
    batches = lax.axis_size("batch")
    if volume.size * 2 * slabs * batches > GATHER_LIMIT or volume.shape[0] % 2:
        return split_body(volume, targets, front_weight, stride_weight, hidden_weight, output_weight)
    inner = front_weight.shape[-1]
    channels = volume.shape[-1]
    features = stride_weight.shape[-1]
    shape = (slabs, batches) + volume.shape + (inner,)
    front_turned = jnp.swapaxes(front_weight.reshape(27, channels, inner), 1, 2)
    stride_own = stride_weight.reshape(27, inner, features)
    gathered, targets, front_other, stride_other, hidden_all = gather_inputs(
        volume, targets, front_turned, stride_own, hidden_weight
    )
    grad_front, grad_stride, grad_hidden, grad_output, loss = whole_batch(
        shape, features, gathered, targets.reshape(-1, targets.shape[-1]),
        front_turned, front_other, stride_own, stride_other, hidden_all, output_weight.T,
    )
    return (
        jnp.swapaxes(grad_front, 1, 2).reshape(3, 3, 3, channels, inner),
        grad_stride.reshape(3, 3, 3, inner, features),
        grad_hidden,
        grad_output.T,
        loss.reshape(1),
    )


def solution(mesh):
    in_specs = (
        P(("groups", "batch"), "slab", None, None, None),
        P(("groups", "batch"), None),
        P(None, None, None, None, "chan"),
        P(None, None, None, "chan", None),
        P("chan", None),
        P(),
    )
    out_specs = (
        P("groups", None, None, None, "chan"),
        P("groups", None, None, "chan", None),
        P(("groups", "chan"), None),
        P("groups", None),
        P("groups"),
    )
    return jax.shard_map(body, mesh=mesh, in_specs=in_specs, out_specs=out_specs, check_vma=False)
```

```python
import functools

import jax
import jax.numpy as jnp
from jax import lax
from jax.experimental import pallas as pl
from jax.experimental.pallas import tpu as pltpu
from jax.sharding import PartitionSpec as P


def with_halo(cells, sides, width):
    for axis, dim in sides:
        count = lax.axis_size(axis)
        ends = count - 1
        head = lax.slice_in_dim(cells, 0, width, axis=dim)
        tail = lax.slice_in_dim(cells, cells.shape[dim] - width, cells.shape[dim], axis=dim)
        cells = jnp.concatenate(
            [
                lax.ppermute(tail, axis, [(i, (i + 1) % count) for i in range(ends)]),
                cells,
                lax.ppermute(head, axis, [((i + 1) % count, i) for i in range(ends)]),
            ],
            axis=dim,
        )
    return cells


def swish_slope(preact):
    logistic = jax.nn.sigmoid(preact)
    return logistic * (1.0 + preact * (1.0 - logistic))


def tap_window(padded, tap_z, tap_x, tap_y, extent_z, extent_x, extent_y, stride):
    if stride == 1:
        return padded[
            :, tap_z : tap_z + extent_z, tap_x : tap_x + extent_x, tap_y : tap_y + extent_y, :
        ]
    leading = padded.shape[0]
    channels = padded.shape[-1]
    folded = padded.reshape(leading, extent_z + 1, 2, extent_x + 1, 2, extent_y + 1, 2, channels)
    return folded[
        :,
        tap_z // 2 : tap_z // 2 + extent_z,
        tap_z % 2,
        tap_x // 2 : tap_x // 2 + extent_x,
        tap_x % 2,
        tap_y // 2 : tap_y // 2 + extent_y,
        tap_y % 2,
        :,
    ]


def conv_apply(padded, weight, extent_z, extent_x, extent_y, stride):
    summed = None
    for tap_z in range(3):
        for tap_x in range(3):
            for tap_y in range(3):
                window = tap_window(
                    padded, tap_z, tap_x, tap_y, extent_z, extent_x, extent_y, stride
                )
                flat_tap = window.reshape(-1, window.shape[-1])
                contrib = jnp.dot(
                    flat_tap, weight[tap_z, tap_x, tap_y], preferred_element_type=jnp.float32
                )
                summed = contrib if summed is None else summed + contrib
    return summed.reshape(padded.shape[0], extent_z, extent_x, extent_y, weight.shape[-1])


def kernel_grad(padded, grad_out, extent_z, extent_x, extent_y, stride):
    flat_grad = grad_out.reshape(-1, grad_out.shape[-1])
    results = []
    for tap_z in range(3):
        for tap_x in range(3):
            for tap_y in range(3):
                window = tap_window(
                    padded, tap_z, tap_x, tap_y, extent_z, extent_x, extent_y, stride
                )
                flat_tap = window.reshape(-1, window.shape[-1])
                results.append(
                    lax.dot_general(
                        flat_tap,
                        flat_grad,
                        (((0,), (0,)), ((), ())),
                        preferred_element_type=jnp.float32,
                    )
                )
    return jnp.stack(results).reshape(3, 3, 3, padded.shape[-1], grad_out.shape[-1])


def input_grad(grad_out, weight, extent_z, extent_x, extent_y):
    leading = grad_out.shape[0]
    channels = weight.shape[3]
    flat_grad = grad_out.reshape(-1, grad_out.shape[-1])
    buckets = {}
    for tap_z in range(3):
        for tap_x in range(3):
            for tap_y in range(3):
                contrib = lax.dot_general(
                    flat_grad,
                    weight[tap_z, tap_x, tap_y],
                    (((1,), (1,)), ((), ())),
                    preferred_element_type=jnp.float32,
                )
                contrib = contrib.reshape(leading, extent_z, extent_x, extent_y, channels)
                placed = jnp.pad(
                    contrib,
                    (
                        (0, 0),
                        (tap_z // 2, 1 - tap_z // 2),
                        (tap_x // 2, 1 - tap_x // 2),
                        (tap_y // 2, 1 - tap_y // 2),
                        (0, 0),
                    ),
                )
                parity = (tap_z % 2, tap_x % 2, tap_y % 2)
                buckets[parity] = placed if parity not in buckets else buckets[parity] + placed
    planes_z = []
    for par_z in range(2):
        planes_x = []
        for par_x in range(2):
            planes_x.append(jnp.stack([buckets[par_z, par_x, par_y] for par_y in range(2)], axis=4))
        planes_z.append(jnp.stack(planes_x, axis=3))
    assembled = jnp.stack(planes_z, axis=2)
    assembled = assembled.reshape(
        leading, 2 * extent_z + 2, 2 * extent_x + 2, 2 * extent_y + 2, channels
    )
    return assembled[:, 1:-1, 1:-1, 1:-1, :]


def split_body(volume, targets, front_weight, stride_weight, hidden_weight, output_weight):
    highest = lax.Precision.HIGHEST
    slabs = lax.axis_size("slab")
    batches = lax.axis_size("batch")
    inner = front_weight.shape[-1]
    leading, thick, extent_x, extent_y, channels = volume.shape
    depth = thick * slabs
    outputs = output_weight.shape[-1]
    haloed = with_halo(volume, (("slab", 1),), 1)
    padded = jnp.pad(haloed, ((0, 0), (0, 0), (1, 1), (1, 1), (0, 0)))
    front_pre = conv_apply(padded, front_weight, thick, extent_x, extent_y, 1)
    front_act = jax.nn.silu(front_pre).astype(jnp.bfloat16)
    merged = front_act.reshape(leading, thick, extent_x, extent_y * inner)
    sample_act = lax.all_to_all(merged, "slab", split_axis=0, concat_axis=1, tiled=True)
    sample_act = sample_act.reshape(1, depth, extent_x, extent_y, inner)
    half_z = depth // 2
    half_x = extent_x // 2
    half_y = extent_y // 2
    cells = half_z * half_x * half_y
    stride_pad = jnp.pad(sample_act, ((0, 0), (1, 1), (1, 1), (1, 1), (0, 0)))
    partial_pre = conv_apply(stride_pad, stride_weight, half_z, half_x, half_y, 2)
    stride_pre = lax.psum_scatter(partial_pre, "chan", scatter_dimension=4, tiled=True)
    pooled = jnp.sum(jax.nn.silu(stride_pre), axis=(0, 1, 2, 3)) / cells
    hidden_pre = lax.psum(jnp.dot(pooled, hidden_weight, precision=highest), "chan")
    hidden_act = jax.nn.silu(hidden_pre)
    predicted = jnp.dot(hidden_act, output_weight, precision=highest)
    target_row = lax.dynamic_index_in_dim(targets, lax.axis_index("slab"), 0, keepdims=False)
    residual = predicted - target_row
    squared = jnp.sum(residual * residual)
    grad_output = jnp.outer(hidden_act, residual)
    grad_hidden_pre = jnp.dot(output_weight, residual, precision=highest) * swish_slope(hidden_pre)
    grad_hidden = jnp.outer(pooled, grad_hidden_pre)
    grad_pooled = jnp.dot(hidden_weight, grad_hidden_pre, precision=highest)
    grad_stride_pre = (grad_pooled / cells * swish_slope(stride_pre)).astype(jnp.bfloat16)
    full_grad = lax.all_gather(grad_stride_pre, "chan", axis=4, tiled=True)
    grad_stride = kernel_grad(stride_pad, full_grad, half_z, half_x, half_y, 2)
    grad_act = input_grad(full_grad, stride_weight, half_z, half_x, half_y).astype(jnp.bfloat16)
    returned = lax.all_to_all(
        grad_act.reshape(1, depth, extent_x, extent_y * inner),
        "slab",
        split_axis=1,
        concat_axis=0,
        tiled=True,
    )
    returned = returned.reshape(leading, thick, extent_x, extent_y, inner)
    grad_front_pre = (returned * swish_slope(front_pre)).astype(jnp.bfloat16)
    grad_front = kernel_grad(padded, grad_front_pre, thick, extent_x, extent_y, 1)
    grad_front, grad_stride, grad_hidden, grad_output, squared = lax.psum(
        (grad_front, grad_stride, grad_hidden, grad_output, squared), ("slab", "batch")
    )
    loss = (squared / (slabs * batches * outputs)).reshape(1)
    return (grad_front, grad_stride, grad_hidden, grad_output, loss)


GATHER_LIMIT = 1 << 20


def whole_kernel(
    shape,
    gathered_hbm, targets_hbm, front_own_hbm, front_other_hbm, stride_own_hbm, stride_other_hbm,
    hidden_hbm, output_hbm,
    grad_front_ref, grad_stride_ref, grad_hidden_ref, grad_output_ref, loss_ref,
    taps_ref, front_ref, act_ref, slope_ref, strided_ref, spread_ref, grad_pre_ref,
    front_out_ref, stride_out_ref, front_sem, stride_sem,
    volume_ref, targets_ref, front_turned_ref, stride_ref, hidden_ref, output_ref, front_pre_ref, fetch_sem,
):
    slabs, batches, leading, thick, extent_x, extent_y, channels, inner = shape
    f32, bf16 = jnp.float32, jnp.bfloat16
    highest = lax.Precision.HIGHEST
    samples = batches * leading
    depth = slabs * thick
    rows = samples * extent_y
    half_z, half_x, half_y = depth // 2, extent_x // 2, extent_y // 2
    half_rows = samples * half_y
    cells = half_z * half_x * half_y
    wide = 3 * channels
    local_rows = leading * extent_y

    fetches = [
        pltpu.make_async_copy(source, target, fetch_sem.at[i])
        for i, (source, target) in enumerate(
            [
                (gathered_hbm, volume_ref),
                (front_own_hbm, front_turned_ref.at[:, pl.ds(0, inner)]),
                (front_other_hbm, front_turned_ref.at[:, pl.ds(inner, inner)]),
                (stride_own_hbm, stride_ref.at[:, pl.ds(0, inner)]),
                (stride_other_hbm, stride_ref.at[:, pl.ds(inner, inner)]),
                (hidden_hbm, hidden_ref),
                (output_hbm, output_ref),
                (targets_hbm, targets_ref),
            ]
        )
    ]
    for fetch in fetches[:3]:
        fetch.start()

    zeros = jnp.zeros((rows, wide), bf16)
    for x in range(extent_x + 2):
        taps_ref[0, x] = zeros
        taps_ref[depth + 1, x] = zeros

    row = lax.broadcasted_iota(jnp.int32, (rows, channels), 0)
    first = (row & (extent_y - 1)) == 0
    last = (row & (extent_y - 1)) == extent_y - 1
    half_row = lax.broadcasted_iota(jnp.int32, (half_rows, channels), 0)
    half_first = (half_row & (half_y - 1)) == 0
    half_last = (half_row & (half_y - 1)) == half_y - 1

    def fill(slab, carry):
        for plane in range(thick):
            z = slab * thick + plane
            taps_ref[z + 1, 0] = zeros
            taps_ref[z + 1, extent_x + 1] = zeros
            for x in range(extent_x):
                mid = jnp.concatenate(
                    [
                        volume_ref[b * slabs + slab, :, plane, x].astype(f32).reshape(local_rows, channels)
                        for b in range(batches)
                    ],
                    axis=0,
                )
                low = jnp.where(first, 0.0, pltpu.roll(mid, 1, 0))
                high = jnp.where(last, 0.0, pltpu.roll(mid, rows - 1, 0))
                taps_ref[z + 1, x + 1, :, :channels] = low.astype(bf16)
                taps_ref[z + 1, x + 1, :, channels : 2 * channels] = mid.astype(bf16)
                taps_ref[z + 1, x + 1, :, 2 * channels :] = high.astype(bf16)
        return carry

    half_zeros = jnp.zeros((half_rows, wide), bf16)
    for x in range(extent_x + 1):
        strided_ref[0, x] = half_zeros
    front_pre_ref[1] = jnp.zeros((extent_x * rows, channels), f32)
    fetches[0].wait()
    for fetch in fetches[3:]:
        fetch.start()
    lax.fori_loop(0, slabs, fill, 0)
    fetches[1].wait()
    fetches[2].wait()
    for kz in range(3):
        for tap in range(9):
            front_ref[tap * channels : (tap + 1) * channels, kz * channels : (kz + 1) * channels] = jnp.transpose(
                front_turned_ref[9 * kz + tap]
            )

    def front_taps(z, carry):
        window = jnp.concatenate(
            [taps_ref[z + 1, kx : kx + extent_x].reshape(extent_x * rows, wide) for kx in range(3)], axis=1
        )
        spread = jnp.dot(window, front_ref[...], preferred_element_type=f32)
        front_pre_ref[z + 2] = spread[:, :channels]
        front_pre_ref[z + 1] += spread[:, channels : 2 * channels]

        @pl.when(z > 0)
        def _():
            front_pre_ref[z] += spread[:, 2 * channels :]

        return carry

    lax.fori_loop(0, depth, front_taps, 0)

    def front(z, carry):
        total = front_pre_ref[z + 1]
        logistic = 1.0 / (1.0 + jnp.exp(-total))
        act = (total * logistic).astype(bf16).astype(f32)
        slope = logistic * (1.0 + total * (1.0 - logistic))
        act_ref[z] = act.reshape(extent_x, rows, channels)
        slope_ref[z] = slope.reshape(extent_x, rows, channels)
        strided_ref[z + 1, 0] = half_zeros
        for x in range(extent_x):
            even = act_ref[z, x, pl.ds(0, half_rows, stride=2), :]
            odd = act_ref[z, x, pl.ds(1, half_rows, stride=2), :]
            low = jnp.where(half_first, 0.0, pltpu.roll(odd, 1, 0))
            strided_ref[z + 1, x + 1, :, :channels] = low.astype(bf16)
            strided_ref[z + 1, x + 1, :, channels : 2 * channels] = even.astype(bf16)
            strided_ref[z + 1, x + 1, :, 2 * channels :] = odd.astype(bf16)
        return carry

    lax.fori_loop(0, depth, front, 0)

    def strided_window(kz, kx):
        return jnp.concatenate(
            [strided_ref[kz + 2 * z, kx + 2 * x] for z in range(half_z) for x in range(half_x)], axis=0
        )

    def stride_kernel(kz, kx):
        start = 3 * (3 * kz + kx)
        return stride_ref[start : start + 3].reshape(wide, stride_ref.shape[-1])

    for fetch in fetches[3:]:
        fetch.wait()
    windows = jnp.concatenate([strided_window(kz, kx) for kz in range(3) for kx in range(3)], axis=1)
    pre = jnp.dot(windows, stride_ref[...].reshape(27 * channels, stride_ref.shape[-1]), preferred_element_type=f32)
    logistic = 1.0 / (1.0 + jnp.exp(-pre))
    planes = half_z * half_x
    features = pre.shape[-1]
    summed = jnp.sum((pre * logistic).reshape(planes, half_rows, features), axis=0)
    owner = lax.broadcasted_iota(jnp.int32, (samples, half_rows), 1)
    sample = lax.broadcasted_iota(jnp.int32, (samples, half_rows), 0)
    member = ((owner >= sample * half_y) & (owner < (sample + 1) * half_y)).astype(f32)
    pooled = jnp.dot(member, summed, precision=highest, preferred_element_type=f32) / cells
    hidden = hidden_ref[...]
    output = output_ref[...]

    def contract(left, right, dims):
        return lax.dot_general(left, right, (dims, ((), ())), precision=highest, preferred_element_type=f32)

    hidden_pre = contract(pooled, hidden, ((1,), (0,)))
    hidden_logistic = 1.0 / (1.0 + jnp.exp(-hidden_pre))
    hidden_act = hidden_pre * hidden_logistic
    residual = contract(hidden_act, output, ((1,), (1,))) - targets_ref[...]
    loss_ref[...] = jnp.sum(residual * residual, keepdims=True) / (samples * output.shape[0])
    grad_output_ref[...] = contract(residual, hidden_act, ((0,), (0,)))
    hidden_slope = hidden_logistic * (1.0 + hidden_pre * (1.0 - hidden_logistic))
    grad_hidden_pre = contract(residual, output, ((1,), (0,))) * hidden_slope
    share = features // 2
    pooled_own = jnp.where(lax.axis_index("chan") == 0, pooled[:, :share], pooled[:, share:])
    grad_hidden_ref[...] = contract(pooled_own, grad_hidden_pre, ((0,), (0,)))
    grad_pooled = contract(grad_hidden_pre, hidden, ((1,), (1,)))
    grad_rows = contract(member, grad_pooled, ((0,), (0,))) / cells
    slope = logistic * (1.0 + pre * (1.0 - logistic))
    grad_pre = (slope.reshape(planes, half_rows, features) * grad_rows[None]).astype(bf16)
    grad_pre = grad_pre.reshape(planes * half_rows, features)

    def send_out(source, target, sems, group):
        place = pl.ds(3 * group, 3)
        return pltpu.make_async_copy(source.at[place], target.at[place], sems.at[group])

    for kz in range(3):
        for kx in range(3):
            start = 3 * (3 * kz + kx)
            kernel = lax.dot_general(
                strided_window(kz, kx), grad_pre, (((0,), (0,)), ((), ())), preferred_element_type=f32
            )
            for ky in range(3):
                stride_out_ref[start + ky] = kernel[ky * channels : ky * channels + inner]
            send_out(stride_out_ref, grad_stride_ref, stride_sem, 3 * kz + kx).start()

    for kz in range(3):
        for kx in range(3):
            spread = lax.dot_general(
                grad_pre, stride_kernel(kz, kx), (((1,), (1,)), ((), ())), preferred_element_type=f32
            )
            spread_ref[3 * kz + kx] = spread.reshape(planes, half_rows, wide)

    def sources(cell, half):
        if cell % 2 == 0:
            return [(1, cell // 2)]
        found = [(2, cell // 2)]
        if cell // 2 + 1 < half:
            found.append((0, cell // 2 + 1))
        return found

    for z in range(depth):
        for x in range(extent_x):
            total = None
            for kz, from_z in sources(z, half_z):
                for kx, from_x in sources(x, half_x):
                    block = spread_ref[3 * kz + kx, from_z * half_x + from_x]
                    total = block if total is None else total + block
            even = total[:, channels : 2 * channels]
            up = jnp.where(half_last, 0.0, pltpu.roll(total[:, :channels], half_rows - 1, 0))
            odd = total[:, 2 * channels :] + up
            for start, grad in ((0, even), (1, odd)):
                grad = grad.astype(bf16).astype(f32)
                place = pl.ds(start, half_rows, stride=2)
                grad_pre_ref[z, x, place, :] = grad * slope_ref[z, x, place, :]

    grads = grad_pre_ref[...].reshape(depth * extent_x * rows, channels).astype(bf16)
    grads = jnp.transpose(grads)[:inner]
    plane_cells = extent_x * rows
    edge = jnp.zeros((inner, plane_cells), bf16)
    stacked = jnp.concatenate(
        [
            jnp.concatenate([grads[:, plane_cells:], edge], axis=1),
            grads,
            jnp.concatenate([edge, grads[:, :-plane_cells]], axis=1),
        ],
        axis=0,
    )
    for kx in range(3):
        window = taps_ref[1 : depth + 1, kx : kx + extent_x].reshape(depth * plane_cells, wide)
        turned = jnp.dot(stacked, window, preferred_element_type=f32)
        for kz in range(3):
            for ky in range(3):
                front_out_ref[3 * (3 * kz + kx) + ky] = turned[
                    kz * inner : (kz + 1) * inner, ky * channels : (ky + 1) * channels
                ]
            send_out(front_out_ref, grad_front_ref, front_sem, 3 * kz + kx).start()
    for group in range(9):
        send_out(stride_out_ref, grad_stride_ref, stride_sem, group).wait()
        send_out(front_out_ref, grad_front_ref, front_sem, group).wait()


def whole_batch(shape, features, gathered, targets, front_own, front_other, stride_own, stride_other, hidden_all, output_turned):
    slabs, batches, leading, thick, extent_x, extent_y, channels, inner = shape
    samples, depth = batches * leading, slabs * thick
    rows = samples * extent_y
    half_rows = rows // 2
    planes = depth * extent_x // 4
    f32, bf16 = jnp.float32, jnp.bfloat16
    outputs, hid = output_turned.shape
    vmem = pl.BlockSpec(memory_space=pltpu.VMEM)
    anywhere = pl.BlockSpec(memory_space=pl.ANY)
    return pl.pallas_call(
        functools.partial(whole_kernel, shape),
        out_shape=(
            jax.ShapeDtypeStruct((27, inner, channels), f32),
            jax.ShapeDtypeStruct((27, inner, features), f32),
            jax.ShapeDtypeStruct((features // 2, hid), f32),
            jax.ShapeDtypeStruct((outputs, hid), f32),
            jax.ShapeDtypeStruct((1, 1), f32),
        ),
        in_specs=[anywhere] * 8,
        out_specs=[anywhere] * 2 + [vmem] * 3,
        scratch_shapes=[
            pltpu.VMEM((depth + 2, extent_x + 2, rows, 3 * channels), bf16),
            pltpu.VMEM((9 * channels, 3 * channels), bf16),
            pltpu.VMEM((depth, extent_x, rows, channels), f32),
            pltpu.VMEM((depth, extent_x, rows, channels), f32),
            pltpu.VMEM((depth + 1, extent_x + 1, half_rows, 3 * channels), bf16),
            pltpu.VMEM((9, planes, half_rows, 3 * channels), f32),
            pltpu.VMEM((depth, extent_x, rows, channels), f32),
            pltpu.VMEM((27, inner, channels), f32),
            pltpu.VMEM((27, inner, features), f32),
            pltpu.SemaphoreType.DMA((9,)),
            pltpu.SemaphoreType.DMA((9,)),
            pltpu.VMEM(gathered.shape, bf16),
            pltpu.VMEM(targets.shape, f32),
            pltpu.VMEM((27, channels, channels), bf16),
            pltpu.VMEM((27, channels, features), bf16),
            pltpu.VMEM(hidden_all.shape, f32),
            pltpu.VMEM(output_turned.shape, f32),
            pltpu.VMEM((depth + 2, extent_x * rows, channels), f32),
            pltpu.SemaphoreType.DMA((8,)),
        ],
        compiler_params=pltpu.CompilerParams(vmem_limit_bytes=60 << 20),
    )(gathered, targets, front_own, front_other, stride_own, stride_other, hidden_all, output_turned)


def gather_kernel(
    slabs, batches,
    volume_ref, targets_ref, front_ref, stride_ref, hidden_ref,
    gathered_ref, targets_all_ref, front_other_ref, stride_other_ref, hidden_all_ref,
    local_sem, slab_sem, batch_sem, piece_sem, pair_send_sem, pair_sem,
    target_send_sem, target_sem, weight_send_sem, weight_sem,
):
    slab, batch, chan = lax.axis_index("slab"), lax.axis_index("batch"), lax.axis_index("chan")
    sibling = {"chan": 1 - chan}
    half = volume_ref.shape[0] // 2
    share = hidden_ref.shape[0]

    def remote(source, target, send_sem, recv_sem, device):
        return pltpu.make_async_remote_copy(
            src_ref=source, dst_ref=target, send_sem=send_sem, recv_sem=recv_sem,
            device_id=device, device_id_type=pl.DeviceIdType.MESH,
        )

    slab_steps = range(1, slabs)
    batch_steps = range(1, batches)
    to_slab = [{"slab": lax.rem(slab + step, slabs)} for step in slab_steps]
    to_batch = [{"batch": lax.rem(batch + step, batches)} for step in batch_steps]
    from_slab = [lax.rem(slab + slabs - step, slabs) for step in slab_steps]
    from_batch = [lax.rem(batch + batches - step, batches) for step in batch_steps]

    barrier = pltpu.get_barrier_semaphore()
    neighbours = to_slab + to_batch + [sibling]
    for device in neighbours:
        pl.semaphore_signal(barrier, inc=1, device_id=device, device_id_type=pl.DeviceIdType.MESH)
    pl.semaphore_wait(barrier, len(neighbours))

    def part(piece, side):
        return gathered_ref.at[piece, pl.ds(side * half, half)]

    mine = batch * slabs + slab
    own = volume_ref.at[pl.ds(chan * half, half)]
    sends = []

    def send(copy):
        copy.start()
        sends.append(copy)

    for i, device in enumerate(to_slab):
        send(remote(own, part(mine, chan), slab_sem.at[i], piece_sem.at[mine], device))
    for i, device in enumerate(to_batch):
        send(remote(own, part(mine, chan), batch_sem.at[0, i], piece_sem.at[mine], device))
        send(remote(targets_ref, targets_all_ref.at[batch], target_send_sem.at[i], target_sem.at[batch], device))
    weights = [
        remote(front_ref, front_other_ref, weight_send_sem.at[0], weight_sem.at[0], sibling),
        remote(stride_ref, stride_other_ref, weight_send_sem.at[1], weight_sem.at[1], sibling),
        remote(hidden_ref, hidden_all_ref.at[pl.ds(chan * share, share)], weight_send_sem.at[2], weight_sem.at[2], sibling),
    ]
    for copy in weights:
        send(copy)
    local = [
        pltpu.make_async_copy(volume_ref, gathered_ref.at[mine], local_sem.at[0]),
        pltpu.make_async_copy(targets_ref, targets_all_ref.at[batch], local_sem.at[1]),
        pltpu.make_async_copy(hidden_ref, hidden_all_ref.at[pl.ds(chan * share, share)], local_sem.at[2]),
    ]
    for copy in local:
        copy.start()

    def arrived(piece, side, sem, device):
        remote(part(piece, side), part(piece, side), slab_sem.at[0], sem.at[piece], device).wait_recv()

    def pass_on(slot, piece):
        send(remote(part(piece, chan), part(piece, chan), pair_send_sem.at[slot], pair_sem.at[piece], sibling))

    slot = 0
    for j, source in enumerate(from_slab):
        piece = batch * slabs + source
        arrived(piece, chan, piece_sem, sibling)
        for i, device in enumerate(to_batch):
            send(remote(part(piece, chan), part(piece, chan), batch_sem.at[j + 1, i], piece_sem.at[piece], device))
        pass_on(slot, piece)
        slot += 1
    for source in from_batch:
        for slab_source in [slab] + from_slab:
            piece = source * slabs + slab_source
            arrived(piece, chan, piece_sem, sibling)
            pass_on(slot, piece)
            slot += 1
        remote(
            targets_ref, targets_all_ref.at[source], target_send_sem.at[0], target_sem.at[source], sibling
        ).wait_recv()
    for source in [batch] + from_batch:
        for slab_source in [slab] + from_slab:
            if source is batch and slab_source is slab:
                continue
            arrived(source * slabs + slab_source, 1 - chan, pair_sem, sibling)
    for copy in weights:
        copy.wait_recv()
    for copy in local:
        copy.wait()
    for copy in sends:
        copy.wait_send()


def gather_inputs(volume, targets, front_turned, stride_own, hidden_weight):
    slabs, batches = lax.axis_size("slab"), lax.axis_size("batch")
    pieces = slabs * batches
    anywhere = pl.BlockSpec(memory_space=pl.ANY)
    share, hid = hidden_weight.shape
    dma = pltpu.SemaphoreType.DMA
    return pl.pallas_call(
        functools.partial(gather_kernel, slabs, batches),
        out_shape=(
            jax.ShapeDtypeStruct((pieces,) + volume.shape, volume.dtype),
            jax.ShapeDtypeStruct((batches,) + targets.shape, targets.dtype),
            jax.ShapeDtypeStruct(front_turned.shape, front_turned.dtype),
            jax.ShapeDtypeStruct(stride_own.shape, stride_own.dtype),
            jax.ShapeDtypeStruct((2 * share, hid), hidden_weight.dtype),
        ),
        in_specs=[anywhere] * 5,
        out_specs=[anywhere] * 5,
        scratch_shapes=[
            dma((3,)), dma((slabs,)), dma((slabs, batches)), dma((pieces,)), dma((pieces,)), dma((pieces,)),
            dma((batches,)), dma((batches,)), dma((3,)), dma((3,)),
        ],
        compiler_params=pltpu.CompilerParams(
            collective_id=0, has_side_effects=True, vmem_limit_bytes=60 << 20
        ),
    )(volume, targets, front_turned, stride_own, hidden_weight)


def body(volume, targets, front_weight, stride_weight, hidden_weight, output_weight):
    slabs = lax.axis_size("slab")
    batches = lax.axis_size("batch")
    if volume.size * 2 * slabs * batches > GATHER_LIMIT or volume.shape[0] % 2:
        return split_body(volume, targets, front_weight, stride_weight, hidden_weight, output_weight)
    inner = front_weight.shape[-1]
    channels = volume.shape[-1]
    features = stride_weight.shape[-1]
    shape = (slabs, batches) + volume.shape + (inner,)
    front_turned = jnp.swapaxes(front_weight.reshape(27, channels, inner), 1, 2)
    stride_own = stride_weight.reshape(27, inner, features)
    gathered, targets, front_other, stride_other, hidden_all = gather_inputs(
        volume, targets, front_turned, stride_own, hidden_weight
    )
    grad_front, grad_stride, grad_hidden, grad_output, loss = whole_batch(
        shape, features, gathered, targets.reshape(-1, targets.shape[-1]),
        front_turned, front_other, stride_own, stride_other, hidden_all, output_weight.T,
    )
    return (
        jnp.swapaxes(grad_front, 1, 2).reshape(3, 3, 3, channels, inner),
        grad_stride.reshape(3, 3, 3, inner, features),
        grad_hidden,
        grad_output.T,
        loss.reshape(1),
    )


def solution(mesh):
    in_specs = (
        P(("groups", "batch"), "slab", None, None, None),
        P(("groups", "batch"), None),
        P(None, None, None, None, "chan"),
        P(None, None, None, "chan", None),
        P("chan", None),
        P(),
    )
    out_specs = (
        P("groups", None, None, None, "chan"),
        P("groups", None, None, "chan", None),
        P(("groups", "chan"), None),
        P("groups", None),
        P("groups"),
    )
    return jax.shard_map(body, mesh=mesh, in_specs=in_specs, out_specs=out_specs, check_vma=False)
```

```python
import functools

import jax
import jax.numpy as jnp
from jax import lax
from jax.experimental import pallas as pl
from jax.experimental.pallas import tpu as pltpu
from jax.sharding import PartitionSpec as P


def with_halo(cells, sides, width):
    for axis, dim in sides:
        count = lax.axis_size(axis)
        ends = count - 1
        head = lax.slice_in_dim(cells, 0, width, axis=dim)
        tail = lax.slice_in_dim(cells, cells.shape[dim] - width, cells.shape[dim], axis=dim)
        cells = jnp.concatenate(
            [
                lax.ppermute(tail, axis, [(i, (i + 1) % count) for i in range(ends)]),
                cells,
                lax.ppermute(head, axis, [((i + 1) % count, i) for i in range(ends)]),
            ],
            axis=dim,
        )
    return cells


def swish_slope(preact):
    logistic = jax.nn.sigmoid(preact)
    return logistic * (1.0 + preact * (1.0 - logistic))


def tap_window(padded, tap_z, tap_x, tap_y, extent_z, extent_x, extent_y, stride):
    if stride == 1:
        return padded[
            :, tap_z : tap_z + extent_z, tap_x : tap_x + extent_x, tap_y : tap_y + extent_y, :
        ]
    leading = padded.shape[0]
    channels = padded.shape[-1]
    folded = padded.reshape(leading, extent_z + 1, 2, extent_x + 1, 2, extent_y + 1, 2, channels)
    return folded[
        :,
        tap_z // 2 : tap_z // 2 + extent_z,
        tap_z % 2,
        tap_x // 2 : tap_x // 2 + extent_x,
        tap_x % 2,
        tap_y // 2 : tap_y // 2 + extent_y,
        tap_y % 2,
        :,
    ]


def conv_apply(padded, weight, extent_z, extent_x, extent_y, stride):
    summed = None
    for tap_z in range(3):
        for tap_x in range(3):
            for tap_y in range(3):
                window = tap_window(
                    padded, tap_z, tap_x, tap_y, extent_z, extent_x, extent_y, stride
                )
                flat_tap = window.reshape(-1, window.shape[-1])
                contrib = jnp.dot(
                    flat_tap, weight[tap_z, tap_x, tap_y], preferred_element_type=jnp.float32
                )
                summed = contrib if summed is None else summed + contrib
    return summed.reshape(padded.shape[0], extent_z, extent_x, extent_y, weight.shape[-1])


def kernel_grad(padded, grad_out, extent_z, extent_x, extent_y, stride):
    flat_grad = grad_out.reshape(-1, grad_out.shape[-1])
    results = []
    for tap_z in range(3):
        for tap_x in range(3):
            for tap_y in range(3):
                window = tap_window(
                    padded, tap_z, tap_x, tap_y, extent_z, extent_x, extent_y, stride
                )
                flat_tap = window.reshape(-1, window.shape[-1])
                results.append(
                    lax.dot_general(
                        flat_tap,
                        flat_grad,
                        (((0,), (0,)), ((), ())),
                        preferred_element_type=jnp.float32,
                    )
                )
    return jnp.stack(results).reshape(3, 3, 3, padded.shape[-1], grad_out.shape[-1])


def input_grad(grad_out, weight, extent_z, extent_x, extent_y):
    leading = grad_out.shape[0]
    channels = weight.shape[3]
    flat_grad = grad_out.reshape(-1, grad_out.shape[-1])
    buckets = {}
    for tap_z in range(3):
        for tap_x in range(3):
            for tap_y in range(3):
                contrib = lax.dot_general(
                    flat_grad,
                    weight[tap_z, tap_x, tap_y],
                    (((1,), (1,)), ((), ())),
                    preferred_element_type=jnp.float32,
                )
                contrib = contrib.reshape(leading, extent_z, extent_x, extent_y, channels)
                placed = jnp.pad(
                    contrib,
                    (
                        (0, 0),
                        (tap_z // 2, 1 - tap_z // 2),
                        (tap_x // 2, 1 - tap_x // 2),
                        (tap_y // 2, 1 - tap_y // 2),
                        (0, 0),
                    ),
                )
                parity = (tap_z % 2, tap_x % 2, tap_y % 2)
                buckets[parity] = placed if parity not in buckets else buckets[parity] + placed
    planes_z = []
    for par_z in range(2):
        planes_x = []
        for par_x in range(2):
            planes_x.append(jnp.stack([buckets[par_z, par_x, par_y] for par_y in range(2)], axis=4))
        planes_z.append(jnp.stack(planes_x, axis=3))
    assembled = jnp.stack(planes_z, axis=2)
    assembled = assembled.reshape(
        leading, 2 * extent_z + 2, 2 * extent_x + 2, 2 * extent_y + 2, channels
    )
    return assembled[:, 1:-1, 1:-1, 1:-1, :]


def split_body(volume, targets, front_weight, stride_weight, hidden_weight, output_weight):
    highest = lax.Precision.HIGHEST
    slabs = lax.axis_size("slab")
    batches = lax.axis_size("batch")
    inner = front_weight.shape[-1]
    leading, thick, extent_x, extent_y, channels = volume.shape
    depth = thick * slabs
    outputs = output_weight.shape[-1]
    haloed = with_halo(volume, (("slab", 1),), 1)
    padded = jnp.pad(haloed, ((0, 0), (0, 0), (1, 1), (1, 1), (0, 0)))
    front_pre = conv_apply(padded, front_weight, thick, extent_x, extent_y, 1)
    front_act = jax.nn.silu(front_pre).astype(jnp.bfloat16)
    merged = front_act.reshape(leading, thick, extent_x, extent_y * inner)
    sample_act = lax.all_to_all(merged, "slab", split_axis=0, concat_axis=1, tiled=True)
    sample_act = sample_act.reshape(1, depth, extent_x, extent_y, inner)
    half_z = depth // 2
    half_x = extent_x // 2
    half_y = extent_y // 2
    cells = half_z * half_x * half_y
    stride_pad = jnp.pad(sample_act, ((0, 0), (1, 1), (1, 1), (1, 1), (0, 0)))
    partial_pre = conv_apply(stride_pad, stride_weight, half_z, half_x, half_y, 2)
    stride_pre = lax.psum_scatter(partial_pre, "chan", scatter_dimension=4, tiled=True)
    pooled = jnp.sum(jax.nn.silu(stride_pre), axis=(0, 1, 2, 3)) / cells
    hidden_pre = lax.psum(jnp.dot(pooled, hidden_weight, precision=highest), "chan")
    hidden_act = jax.nn.silu(hidden_pre)
    predicted = jnp.dot(hidden_act, output_weight, precision=highest)
    target_row = lax.dynamic_index_in_dim(targets, lax.axis_index("slab"), 0, keepdims=False)
    residual = predicted - target_row
    squared = jnp.sum(residual * residual)
    grad_output = jnp.outer(hidden_act, residual)
    grad_hidden_pre = jnp.dot(output_weight, residual, precision=highest) * swish_slope(hidden_pre)
    grad_hidden = jnp.outer(pooled, grad_hidden_pre)
    grad_pooled = jnp.dot(hidden_weight, grad_hidden_pre, precision=highest)
    grad_stride_pre = (grad_pooled / cells * swish_slope(stride_pre)).astype(jnp.bfloat16)
    full_grad = lax.all_gather(grad_stride_pre, "chan", axis=4, tiled=True)
    grad_stride = kernel_grad(stride_pad, full_grad, half_z, half_x, half_y, 2)
    grad_act = input_grad(full_grad, stride_weight, half_z, half_x, half_y).astype(jnp.bfloat16)
    returned = lax.all_to_all(
        grad_act.reshape(1, depth, extent_x, extent_y * inner),
        "slab",
        split_axis=1,
        concat_axis=0,
        tiled=True,
    )
    returned = returned.reshape(leading, thick, extent_x, extent_y, inner)
    grad_front_pre = (returned * swish_slope(front_pre)).astype(jnp.bfloat16)
    grad_front = kernel_grad(padded, grad_front_pre, thick, extent_x, extent_y, 1)
    grad_front, grad_stride, grad_hidden, grad_output, squared = lax.psum(
        (grad_front, grad_stride, grad_hidden, grad_output, squared), ("slab", "batch")
    )
    loss = (squared / (slabs * batches * outputs)).reshape(1)
    return (grad_front, grad_stride, grad_hidden, grad_output, loss)


GATHER_LIMIT = 1 << 20


def whole_kernel(
    shape,
    gathered_hbm, targets_hbm, front_own_hbm, front_other_hbm, stride_own_hbm, stride_other_hbm,
    hidden_hbm, output_hbm,
    grad_front_ref, grad_stride_ref, grad_hidden_ref, grad_output_ref, loss_ref,
    taps_ref, front_ref, act_ref, slope_ref, strided_ref, spread_ref, grad_pre_ref,
    front_out_ref, stride_out_ref, front_sem, stride_sem,
    volume_ref, targets_ref, front_turned_ref, stride_ref, hidden_ref, output_ref, front_pre_ref, fetch_sem,
):
    slabs, batches, leading, thick, extent_x, extent_y, channels, inner = shape
    f32, bf16 = jnp.float32, jnp.bfloat16
    highest = lax.Precision.HIGHEST
    samples = batches * leading
    depth = slabs * thick
    rows = samples * extent_y
    half_z, half_x, half_y = depth // 2, extent_x // 2, extent_y // 2
    half_rows = samples * half_y
    cells = half_z * half_x * half_y
    wide = 3 * channels
    local_rows = leading * extent_y

    fetches = [
        pltpu.make_async_copy(source, target, fetch_sem.at[i])
        for i, (source, target) in enumerate(
            [
                (gathered_hbm, volume_ref),
                (front_own_hbm, front_turned_ref.at[:, pl.ds(0, inner)]),
                (front_other_hbm, front_turned_ref.at[:, pl.ds(inner, inner)]),
                (stride_own_hbm, stride_ref.at[:, pl.ds(0, inner)]),
                (stride_other_hbm, stride_ref.at[:, pl.ds(inner, inner)]),
                (hidden_hbm, hidden_ref),
                (output_hbm, output_ref),
                (targets_hbm, targets_ref),
            ]
        )
    ]
    for fetch in fetches[:3]:
        fetch.start()

    zeros = jnp.zeros((rows, wide), bf16)
    for x in range(extent_x + 2):
        taps_ref[0, x] = zeros
        taps_ref[depth + 1, x] = zeros

    row = lax.broadcasted_iota(jnp.int32, (rows, channels), 0)
    first = (row & (extent_y - 1)) == 0
    last = (row & (extent_y - 1)) == extent_y - 1
    half_row = lax.broadcasted_iota(jnp.int32, (half_rows, channels), 0)
    half_first = (half_row & (half_y - 1)) == 0
    half_last = (half_row & (half_y - 1)) == half_y - 1

    def fill(slab, carry):
        for plane in range(thick):
            z = slab * thick + plane
            taps_ref[z + 1, 0] = zeros
            taps_ref[z + 1, extent_x + 1] = zeros
            for x in range(extent_x):
                mid = jnp.concatenate(
                    [
                        volume_ref[b * slabs + slab, :, plane, x].astype(f32).reshape(local_rows, channels)
                        for b in range(batches)
                    ],
                    axis=0,
                )
                low = jnp.where(first, 0.0, pltpu.roll(mid, 1, 0))
                high = jnp.where(last, 0.0, pltpu.roll(mid, rows - 1, 0))
                taps_ref[z + 1, x + 1, :, :channels] = low.astype(bf16)
                taps_ref[z + 1, x + 1, :, channels : 2 * channels] = mid.astype(bf16)
                taps_ref[z + 1, x + 1, :, 2 * channels :] = high.astype(bf16)
        return carry

    half_zeros = jnp.zeros((half_rows, wide), bf16)
    for x in range(extent_x + 1):
        strided_ref[0, x] = half_zeros
    front_pre_ref[1] = jnp.zeros((extent_x * rows, channels), f32)
    fetches[0].wait()
    for fetch in fetches[3:]:
        fetch.start()
    lax.fori_loop(0, slabs, fill, 0)
    fetches[1].wait()
    fetches[2].wait()
    for kz in range(3):
        for tap in range(9):
            front_ref[tap * channels : (tap + 1) * channels, kz * channels : (kz + 1) * channels] = jnp.transpose(
                front_turned_ref[9 * kz + tap]
            )

    def front_taps(z, carry):
        window = jnp.concatenate(
            [taps_ref[z + 1, kx : kx + extent_x].reshape(extent_x * rows, wide) for kx in range(3)], axis=1
        )
        spread = jnp.dot(window, front_ref[...], preferred_element_type=f32)
        front_pre_ref[z + 2] = spread[:, :channels]
        front_pre_ref[z + 1] += spread[:, channels : 2 * channels]

        @pl.when(z > 0)
        def _():
            front_pre_ref[z] += spread[:, 2 * channels :]

        return carry

    lax.fori_loop(0, depth, front_taps, 0)

    def front(z, carry):
        total = front_pre_ref[z + 1]
        logistic = 1.0 / (1.0 + jnp.exp(-total))
        act = (total * logistic).astype(bf16).astype(f32)
        slope = logistic * (1.0 + total * (1.0 - logistic))
        act_ref[z] = act.reshape(extent_x, rows, channels)
        slope_ref[z] = slope.reshape(extent_x, rows, channels)
        strided_ref[z + 1, 0] = half_zeros
        for x in range(extent_x):
            even = act_ref[z, x, pl.ds(0, half_rows, stride=2), :]
            odd = act_ref[z, x, pl.ds(1, half_rows, stride=2), :]
            low = jnp.where(half_first, 0.0, pltpu.roll(odd, 1, 0))
            strided_ref[z + 1, x + 1, :, :channels] = low.astype(bf16)
            strided_ref[z + 1, x + 1, :, channels : 2 * channels] = even.astype(bf16)
            strided_ref[z + 1, x + 1, :, 2 * channels :] = odd.astype(bf16)
        return carry

    lax.fori_loop(0, depth, front, 0)

    def strided_window(kz, kx):
        return jnp.concatenate(
            [strided_ref[kz + 2 * z, kx + 2 * x] for z in range(half_z) for x in range(half_x)], axis=0
        )

    def stride_kernel(kz, kx):
        start = 3 * (3 * kz + kx)
        return stride_ref[start : start + 3].reshape(wide, stride_ref.shape[-1])

    for fetch in fetches[3:]:
        fetch.wait()
    windows = jnp.concatenate([strided_window(kz, kx) for kz in range(3) for kx in range(3)], axis=1)
    pre = jnp.dot(windows, stride_ref[...].reshape(27 * channels, stride_ref.shape[-1]), preferred_element_type=f32)
    logistic = 1.0 / (1.0 + jnp.exp(-pre))
    planes = half_z * half_x
    features = pre.shape[-1]
    summed = jnp.sum((pre * logistic).reshape(planes, half_rows, features), axis=0)
    owner = lax.broadcasted_iota(jnp.int32, (samples, half_rows), 1)
    sample = lax.broadcasted_iota(jnp.int32, (samples, half_rows), 0)
    member = ((owner >= sample * half_y) & (owner < (sample + 1) * half_y)).astype(f32)
    pooled = jnp.dot(member, summed, precision=highest, preferred_element_type=f32) / cells
    hidden = hidden_ref[...]
    output = output_ref[...]

    def contract(left, right, dims):
        return lax.dot_general(left, right, (dims, ((), ())), precision=highest, preferred_element_type=f32)

    hidden_pre = contract(pooled, hidden, ((1,), (0,)))
    hidden_logistic = 1.0 / (1.0 + jnp.exp(-hidden_pre))
    hidden_act = hidden_pre * hidden_logistic
    residual = contract(hidden_act, output, ((1,), (1,))) - targets_ref[...]
    loss_ref[...] = jnp.sum(residual * residual, keepdims=True) / (samples * output.shape[0])
    grad_output_ref[...] = contract(residual, hidden_act, ((0,), (0,)))
    hidden_slope = hidden_logistic * (1.0 + hidden_pre * (1.0 - hidden_logistic))
    grad_hidden_pre = contract(residual, output, ((1,), (0,))) * hidden_slope
    share = features // 2
    pooled_own = jnp.where(lax.axis_index("chan") == 0, pooled[:, :share], pooled[:, share:])
    grad_hidden_ref[...] = contract(pooled_own, grad_hidden_pre, ((0,), (0,)))
    grad_pooled = contract(grad_hidden_pre, hidden, ((1,), (1,)))
    grad_rows = contract(member, grad_pooled, ((0,), (0,))) / cells
    slope = logistic * (1.0 + pre * (1.0 - logistic))
    grad_pre = (slope.reshape(planes, half_rows, features) * grad_rows[None]).astype(bf16)
    grad_pre = grad_pre.reshape(planes * half_rows, features)

    def send_out(source, target, sems, group):
        place = pl.ds(3 * group, 3)
        return pltpu.make_async_copy(source.at[place], target.at[place], sems.at[group])

    for kz in range(3):
        for kx in range(3):
            start = 3 * (3 * kz + kx)
            kernel = lax.dot_general(
                strided_window(kz, kx), grad_pre, (((0,), (0,)), ((), ())), preferred_element_type=f32
            )
            for ky in range(3):
                stride_out_ref[start + ky] = kernel[ky * channels : ky * channels + inner]
            send_out(stride_out_ref, grad_stride_ref, stride_sem, 3 * kz + kx).start()

    for kz in range(3):
        for kx in range(3):
            spread = lax.dot_general(
                grad_pre, stride_kernel(kz, kx), (((1,), (1,)), ((), ())), preferred_element_type=f32
            )
            spread_ref[3 * kz + kx] = spread.reshape(planes, half_rows, wide)

    def sources(cell, half):
        if cell % 2 == 0:
            return [(1, cell // 2)]
        found = [(2, cell // 2)]
        if cell // 2 + 1 < half:
            found.append((0, cell // 2 + 1))
        return found

    for z in range(depth):
        for x in range(extent_x):
            total = None
            for kz, from_z in sources(z, half_z):
                for kx, from_x in sources(x, half_x):
                    block = spread_ref[3 * kz + kx, from_z * half_x + from_x]
                    total = block if total is None else total + block
            even = total[:, channels : 2 * channels]
            up = jnp.where(half_last, 0.0, pltpu.roll(total[:, :channels], half_rows - 1, 0))
            odd = total[:, 2 * channels :] + up
            for start, grad in ((0, even), (1, odd)):
                grad = grad.astype(bf16).astype(f32)
                place = pl.ds(start, half_rows, stride=2)
                grad_pre_ref[z, x, place, :] = grad * slope_ref[z, x, place, :]

    grads = grad_pre_ref[...].reshape(depth * extent_x * rows, channels).astype(bf16)
    grads = jnp.transpose(grads)[:inner]
    plane_cells = extent_x * rows
    edge = jnp.zeros((inner, plane_cells), bf16)
    stacked = jnp.concatenate(
        [
            jnp.concatenate([grads[:, plane_cells:], edge], axis=1),
            grads,
            jnp.concatenate([edge, grads[:, :-plane_cells]], axis=1),
        ],
        axis=0,
    )
    for kx in range(3):
        window = taps_ref[1 : depth + 1, kx : kx + extent_x].reshape(depth * plane_cells, wide)
        turned = jnp.dot(stacked, window, preferred_element_type=f32)
        for kz in range(3):
            for ky in range(3):
                front_out_ref[3 * (3 * kz + kx) + ky] = turned[
                    kz * inner : (kz + 1) * inner, ky * channels : (ky + 1) * channels
                ]
            send_out(front_out_ref, grad_front_ref, front_sem, 3 * kz + kx).start()
    for group in range(9):
        send_out(stride_out_ref, grad_stride_ref, stride_sem, group).wait()
        send_out(front_out_ref, grad_front_ref, front_sem, group).wait()


def whole_batch(shape, features, gathered, targets, front_own, front_other, stride_own, stride_other, hidden_all, output_turned):
    slabs, batches, leading, thick, extent_x, extent_y, channels, inner = shape
    samples, depth = batches * leading, slabs * thick
    rows = samples * extent_y
    half_rows = rows // 2
    planes = depth * extent_x // 4
    f32, bf16 = jnp.float32, jnp.bfloat16
    outputs, hid = output_turned.shape
    vmem = pl.BlockSpec(memory_space=pltpu.VMEM)
    anywhere = pl.BlockSpec(memory_space=pl.ANY)
    return pl.pallas_call(
        functools.partial(whole_kernel, shape),
        out_shape=(
            jax.ShapeDtypeStruct((27, inner, channels), f32),
            jax.ShapeDtypeStruct((27, inner, features), f32),
            jax.ShapeDtypeStruct((features // 2, hid), f32),
            jax.ShapeDtypeStruct((outputs, hid), f32),
            jax.ShapeDtypeStruct((1, 1), f32),
        ),
        in_specs=[anywhere] * 8,
        out_specs=[anywhere] * 2 + [vmem] * 3,
        scratch_shapes=[
            pltpu.VMEM((depth + 2, extent_x + 2, rows, 3 * channels), bf16),
            pltpu.VMEM((9 * channels, 3 * channels), bf16),
            pltpu.VMEM((depth, extent_x, rows, channels), f32),
            pltpu.VMEM((depth, extent_x, rows, channels), f32),
            pltpu.VMEM((depth + 1, extent_x + 1, half_rows, 3 * channels), bf16),
            pltpu.VMEM((9, planes, half_rows, 3 * channels), f32),
            pltpu.VMEM((depth, extent_x, rows, channels), f32),
            pltpu.VMEM((27, inner, channels), f32),
            pltpu.VMEM((27, inner, features), f32),
            pltpu.SemaphoreType.DMA((9,)),
            pltpu.SemaphoreType.DMA((9,)),
            pltpu.VMEM(gathered.shape, bf16),
            pltpu.VMEM(targets.shape, f32),
            pltpu.VMEM((27, channels, channels), bf16),
            pltpu.VMEM((27, channels, features), bf16),
            pltpu.VMEM(hidden_all.shape, f32),
            pltpu.VMEM(output_turned.shape, f32),
            pltpu.VMEM((depth + 2, extent_x * rows, channels), f32),
            pltpu.SemaphoreType.DMA((8,)),
        ],
        compiler_params=pltpu.CompilerParams(vmem_limit_bytes=60 << 20),
    )(gathered, targets, front_own, front_other, stride_own, stride_other, hidden_all, output_turned)


def partners(me, step, count):
    if count & (count - 1):
        return lax.rem(me + step, count), lax.rem(me + count - step, count)
    other, bit = me, 1
    while bit < count:
        if step & bit:
            other = other + bit - 2 * bit * ((me // bit) % 2)
        bit *= 2
    return other, other


def gather_kernel(
    slabs, batches,
    volume_ref, targets_ref, front_ref, stride_ref, hidden_ref,
    gathered_ref, targets_all_ref, front_other_ref, stride_other_ref, hidden_all_ref,
    local_sem, slab_sem, batch_sem, piece_sem, pair_send_sem, pair_sem,
    target_send_sem, target_sem, weight_send_sem, weight_sem,
):
    slab, batch, chan = lax.axis_index("slab"), lax.axis_index("batch"), lax.axis_index("chan")
    sibling = {"chan": 1 - chan}
    half = volume_ref.shape[0] // 2
    share = hidden_ref.shape[0]

    def remote(source, target, send_sem, recv_sem, device):
        return pltpu.make_async_remote_copy(
            src_ref=source, dst_ref=target, send_sem=send_sem, recv_sem=recv_sem,
            device_id=device, device_id_type=pl.DeviceIdType.MESH,
        )

    slab_steps = range(1, slabs)
    batch_steps = range(1, batches)
    to_slab = [{"slab": partners(slab, step, slabs)[0]} for step in slab_steps]
    to_batch = [{"batch": lax.rem(batch + step, batches)} for step in batch_steps]
    from_slab = [partners(slab, step, slabs)[1] for step in slab_steps]
    from_batch = [lax.rem(batch + batches - step, batches) for step in batch_steps]

    barrier = pltpu.get_barrier_semaphore()
    neighbours = to_slab + to_batch + [sibling]
    for device in neighbours:
        pl.semaphore_signal(barrier, inc=1, device_id=device, device_id_type=pl.DeviceIdType.MESH)
    pl.semaphore_wait(barrier, len(neighbours))

    def part(piece, side):
        return gathered_ref.at[piece, pl.ds(side * half, half)]

    mine = batch * slabs + slab
    own = volume_ref.at[pl.ds(chan * half, half)]
    sends = []

    def send(copy):
        copy.start()
        sends.append(copy)

    for i, device in enumerate(to_slab):
        send(remote(own, part(mine, chan), slab_sem.at[i], piece_sem.at[mine], device))
    for i, device in enumerate(to_batch):
        send(remote(own, part(mine, chan), batch_sem.at[0, i], piece_sem.at[mine], device))
        send(remote(targets_ref, targets_all_ref.at[batch], target_send_sem.at[i], target_sem.at[batch], device))
    weights = [
        remote(front_ref, front_other_ref, weight_send_sem.at[0], weight_sem.at[0], sibling),
        remote(stride_ref, stride_other_ref, weight_send_sem.at[1], weight_sem.at[1], sibling),
        remote(hidden_ref, hidden_all_ref.at[pl.ds(chan * share, share)], weight_send_sem.at[2], weight_sem.at[2], sibling),
    ]
    for copy in weights:
        send(copy)
    local = [
        pltpu.make_async_copy(volume_ref, gathered_ref.at[mine], local_sem.at[0]),
        pltpu.make_async_copy(targets_ref, targets_all_ref.at[batch], local_sem.at[1]),
        pltpu.make_async_copy(hidden_ref, hidden_all_ref.at[pl.ds(chan * share, share)], local_sem.at[2]),
    ]
    for copy in local:
        copy.start()

    def arrived(piece, side, sem, device):
        remote(part(piece, side), part(piece, side), slab_sem.at[0], sem.at[piece], device).wait_recv()

    def pass_on(slot, piece):
        send(remote(part(piece, chan), part(piece, chan), pair_send_sem.at[slot], pair_sem.at[piece], sibling))

    slot = 0
    for j, source in enumerate(from_slab):
        piece = batch * slabs + source
        arrived(piece, chan, piece_sem, sibling)
        for i, device in enumerate(to_batch):
            send(remote(part(piece, chan), part(piece, chan), batch_sem.at[j + 1, i], piece_sem.at[piece], device))
        pass_on(slot, piece)
        slot += 1
    for source in from_batch:
        for slab_source in [slab] + from_slab:
            piece = source * slabs + slab_source
            arrived(piece, chan, piece_sem, sibling)
            pass_on(slot, piece)
            slot += 1
        remote(
            targets_ref, targets_all_ref.at[source], target_send_sem.at[0], target_sem.at[source], sibling
        ).wait_recv()
    for source in [batch] + from_batch:
        for slab_source in [slab] + from_slab:
            if source is batch and slab_source is slab:
                continue
            arrived(source * slabs + slab_source, 1 - chan, pair_sem, sibling)
    for copy in weights:
        copy.wait_recv()
    for copy in local:
        copy.wait()
    for copy in sends:
        copy.wait_send()


def gather_inputs(volume, targets, front_turned, stride_own, hidden_weight):
    slabs, batches = lax.axis_size("slab"), lax.axis_size("batch")
    pieces = slabs * batches
    anywhere = pl.BlockSpec(memory_space=pl.ANY)
    share, hid = hidden_weight.shape
    dma = pltpu.SemaphoreType.DMA
    return pl.pallas_call(
        functools.partial(gather_kernel, slabs, batches),
        out_shape=(
            jax.ShapeDtypeStruct((pieces,) + volume.shape, volume.dtype),
            jax.ShapeDtypeStruct((batches,) + targets.shape, targets.dtype),
            jax.ShapeDtypeStruct(front_turned.shape, front_turned.dtype),
            jax.ShapeDtypeStruct(stride_own.shape, stride_own.dtype),
            jax.ShapeDtypeStruct((2 * share, hid), hidden_weight.dtype),
        ),
        in_specs=[anywhere] * 5,
        out_specs=[anywhere] * 5,
        scratch_shapes=[
            dma((3,)), dma((slabs,)), dma((slabs, batches)), dma((pieces,)), dma((pieces,)), dma((pieces,)),
            dma((batches,)), dma((batches,)), dma((3,)), dma((3,)),
        ],
        compiler_params=pltpu.CompilerParams(
            collective_id=0, has_side_effects=True, vmem_limit_bytes=60 << 20
        ),
    )(volume, targets, front_turned, stride_own, hidden_weight)


def body(volume, targets, front_weight, stride_weight, hidden_weight, output_weight):
    slabs = lax.axis_size("slab")
    batches = lax.axis_size("batch")
    if volume.size * 2 * slabs * batches > GATHER_LIMIT or volume.shape[0] % 2:
        return split_body(volume, targets, front_weight, stride_weight, hidden_weight, output_weight)
    inner = front_weight.shape[-1]
    channels = volume.shape[-1]
    features = stride_weight.shape[-1]
    shape = (slabs, batches) + volume.shape + (inner,)
    front_turned = jnp.swapaxes(front_weight.reshape(27, channels, inner), 1, 2)
    stride_own = stride_weight.reshape(27, inner, features)
    gathered, targets, front_other, stride_other, hidden_all = gather_inputs(
        volume, targets, front_turned, stride_own, hidden_weight
    )
    grad_front, grad_stride, grad_hidden, grad_output, loss = whole_batch(
        shape, features, gathered, targets.reshape(-1, targets.shape[-1]),
        front_turned, front_other, stride_own, stride_other, hidden_all, output_weight.T,
    )
    return (
        jnp.swapaxes(grad_front, 1, 2).reshape(3, 3, 3, channels, inner),
        grad_stride.reshape(3, 3, 3, inner, features),
        grad_hidden,
        grad_output.T,
        loss.reshape(1),
    )


def solution(mesh):
    in_specs = (
        P(("groups", "batch"), "slab", None, None, None),
        P(("groups", "batch"), None),
        P(None, None, None, None, "chan"),
        P(None, None, None, "chan", None),
        P("chan", None),
        P(),
    )
    out_specs = (
        P("groups", None, None, None, "chan"),
        P("groups", None, None, "chan", None),
        P(("groups", "chan"), None),
        P("groups", None),
        P("groups"),
    )
    return jax.shard_map(body, mesh=mesh, in_specs=in_specs, out_specs=out_specs, check_vma=False)
```
